32 devices in a mesh: lat: 8 (over y, x, core), lon: 4 (over z).
Axes of the slice: x: 2, y: 2, z: 4, core: 2. Of those that a mesh axis runs over, the one named last changes fastest.
Arguments:
- snapshots: float32 [1024, 128, 512], P(None, 'lat', 'lon'), may hold values from -60 to 60
- land_sea: int32 [128, 512], P('lat', 'lon'), may hold values 0 or 1
- penalty: float32 [128, 512], P('lat', 'lon'), may hold values from 0.003 to 0.03
- initial_basis: float32 [64, 128, 512], P(None, 'lat', 'lon'), may hold values from -6 to 6
Outputs:
- leading_basis: float32 [64, 128, 512], P(None, 'lat', 'lon')
- rayleigh_matrix: float32 [64, 64], replicated
The draws below stay inside these ranges and needn't reach their ends.
All inputs are finite; a program needn't handle non-finite values. No bound on the sum of `land_sea` on one device may be relied on, other than what follows from the above.
Results may differ from the reference program's by a relative error of at most 0.0003.
Values sent between devices are 32-bit elements; how exact they have to be, the bound alone decides.
A program may use at most 64 MiB of HBM per device.

```python
import math
import jax
import jax.numpy as jnp
from jax import lax

K = 64
NSNAP = 1024
STEPS = 2
NLAT = 128
NLON = 512
NPTS = 65536


def draw_snapshots(key, part):
    streams = jax.random.split(jax.random.fold_in(key, 7), 9)
    snapshot_scale = 10.0 ** jax.random.uniform(streams[0], (NSNAP, 1, 1), dtype=jnp.float32) / 4.637
    point_scale = 10.0 ** jax.random.uniform(streams[1], (1, NLAT, NLON), dtype=jnp.float32) / 4.637
    latitude_ramp = (1.0 + 2.0 * jnp.arange(NLAT, dtype=jnp.float32) / max(NLAT - 1, 1)).reshape(1, NLAT, 1) / 2.082
    lat_frac = (jnp.arange(NLAT, dtype=jnp.float32) / NLAT).reshape(1, NLAT, 1)
    lon_frac = (jnp.arange(NLON, dtype=jnp.float32) / NLON).reshape(1, 1, NLON)
    wave_lat = jax.random.randint(streams[4], (4,), 1, 5).astype(jnp.float32)
    wave_lon = jax.random.randint(streams[5], (4,), 1, 5).astype(jnp.float32)
    phases = jax.random.uniform(streams[6], (4,), dtype=jnp.float32, minval=0.0, maxval=2.0 * math.pi)
    strength = 6.0 * 5.0 ** jax.random.uniform(streams[7], (4,), dtype=jnp.float32)
    amplitude = jnp.sqrt(2.0 * strength / NSNAP)
    series = jnp.clip(jax.random.normal(streams[8], (4, NSNAP), dtype=jnp.float32), -3.0, 3.0)
    modes_sum = jnp.zeros((NSNAP, NLAT, NLON), jnp.float32)
    for mode in range(4):
        pattern = jnp.cos(2.0 * math.pi * (wave_lat[mode] * lat_frac + wave_lon[mode] * lon_frac) + phases[mode])
        modes_sum = modes_sum + (amplitude[mode] * series[mode]).reshape(NSNAP, 1, 1) * pattern
    values = jnp.clip(jax.random.normal(streams[2], (NSNAP, NLAT, NLON), dtype=jnp.float32), -6.0, 6.0)
    return ((values * snapshot_scale * point_scale + modes_sum) * latitude_ramp).astype(jnp.float32)


def place_ends(entries, own_key, low, high):
    spot = [jax.random.randint(jax.random.fold_in(own_key, axis), (), 0, length) for axis, length in enumerate(entries.shape)]
    longest = entries.shape.index(max(entries.shape))
    next_to = spot[:longest] + [(spot[longest] + 1) % entries.shape[longest]] + spot[longest + 1:]
    return entries.at[tuple(spot)].set(low).at[tuple(next_to)].set(high)


def shard_levels(key, extent, cuts, least, largest):
    level, own = 1.0, jax.random.fold_in(key, 6)
    for position, blocks in cuts:
        steps = jnp.exp(jax.random.uniform(jax.random.fold_in(own, position), (blocks,), jnp.float32, least / len(cuts), largest / len(cuts)))
        level = level * jnp.repeat(steps, extent[position] // blocks).reshape([-1 if axis == position else 1 for axis in range(len(extent))])
    return level


def centred(stream_key, shape, spread, most, cuts=(), held_as=jnp.bfloat16):
    entries = spread * jax.random.normal(stream_key, shape, jnp.float32)
    if cuts:
        entries = entries * shard_levels(stream_key, shape, cuts, -0.22, 0.18)
    return jnp.clip(entries, -most, most).astype(held_as)


def setup_inputs(seed: int = 0) -> dict:
    arg_keys = jax.random.split(jax.random.key(seed), 5)
    return {
        "snapshots": draw_snapshots(jax.random.fold_in(arg_keys[4], 71), 0),
        "land_sea": place_ends((jax.random.randint(arg_keys[1], (NLAT, NLON), 0, 4) < 3).astype(jnp.int32), jax.random.fold_in(arg_keys[1], 1), 0, 1),
        "penalty": jnp.clip(jnp.exp(math.log(0.03) - 2.3025851 * jax.random.uniform(arg_keys[2], (NLAT, NLON), jnp.float32) ** shard_levels(arg_keys[2], (NLAT, NLON), ((0, 8), (1, 4)), -0.2, 0.2)), 0.003, 0.03),
        "initial_basis": centred(arg_keys[3], (K, NLAT, NLON), 1.0, 6.0, ((1, 8), (2, 4)), jnp.float32),
    }


def apply_operator(current_basis, snapshots, ocean_mask, penalty):
    masked_field = current_basis * ocean_mask
    coeffs = jnp.einsum('tab,kab->tk', snapshots, masked_field, precision=lax.Precision.HIGHEST)
    expanded = jnp.einsum('tab,tk->kab', snapshots, coeffs, precision=lax.Precision.HIGHEST)
    padded = jnp.pad(masked_field, ((0, 0), (1, 1), (1, 1)))
    neighbours = padded[:, 2:, 1:-1] + padded[:, :-2, 1:-1] + padded[:, 1:-1, 2:] + padded[:, 1:-1, :-2]
    return ocean_mask * (expanded / NPTS + penalty * (neighbours - 4.0 * masked_field))

def inner_products(left_field, right_field):
    return jnp.einsum('kab,jab->kj', left_field, right_field, precision=lax.Precision.HIGHEST)

def reference(snapshots, land_sea, penalty, initial_basis):
    ocean_mask = land_sea.astype(jnp.float32)
    current_basis = initial_basis * ocean_mask
    for iteration in range(STEPS):
        applied = apply_operator(current_basis, snapshots, ocean_mask, penalty)
        moments = inner_products(applied, applied) / NPTS
        factor = jnp.linalg.cholesky(moments)
        solved = jax.scipy.linalg.solve_triangular(factor, applied.reshape(K, -1), lower=True)
        current_basis = solved.reshape(applied.shape)
    final_image = apply_operator(current_basis, snapshots, ocean_mask, penalty)
    rayleigh_matrix = inner_products(current_basis, final_image) / NPTS
    return (current_basis, rayleigh_matrix)
```

```python
import functools

import jax
import jax.numpy as jnp
from jax import lax
from jax.experimental import pallas as pl
from jax.experimental.pallas import tpu as pltpu
from jax.sharding import PartitionSpec as P

STEPS = 2
MESH = pl.DeviceIdType.MESH
F32 = jnp.float32
BF16 = jnp.bfloat16
NT = (((1,), (1,)), ((), ()))
NN = (((1,), (0,)), ((), ()))


def dot_low(a, b, dims):
    return lax.dot_general(a, b, dims, preferred_element_type=F32)


def dot_full(a, b, dims):
    return lax.dot_general(
        a, b, dims, precision=lax.Precision.HIGHEST, preferred_element_type=F32
    )


def split(x):
    high = x.astype(BF16)
    return high, (x - high.astype(F32)).astype(BF16)


def split3(x):
    high = x.astype(BF16)
    rest = x - high.astype(F32)
    mid = rest.astype(BF16)
    return jnp.concatenate([high, mid, (rest - mid.astype(F32)).astype(BF16)], axis=0)


def fold_rows(x, k):
    return x[:k] + (x[k:2 * k] + x[2 * k:])


def products(left, right):
    k = left.shape[0] // 3
    x = fold_rows(dot_low(left, right, NT), k)
    return x[:, :k] + (x[:, k:2 * k] + x[:, 2 * k:])


def factor_parts(inverse):
    k = inverse.shape[0]
    parts = split3(inverse)
    return jnp.concatenate([parts, parts, parts], axis=1)


def times(parts, right):
    return fold_rows(dot_low(parts, right, NN), parts.shape[0] // 3)


def inverse_factor(gram):
    k = gram.shape[0]
    panel = 4
    rows = lax.broadcasted_iota(jnp.int32, (k, k), 0)
    cols = lax.broadcasted_iota(jnp.int32, (k, k), 1)
    eye = jnp.where(rows == cols, 1.0, 0.0).astype(F32)
    work = jnp.concatenate([gram, eye], axis=1)
    count = k // 8
    shape = (8, 2 * k)
    blocks = [work[8 * i:8 * i + 8] for i in range(count)]
    sub = lax.broadcasted_iota(jnp.int32, shape, 0)
    pivots = [jnp.zeros(shape, F32) for _ in range(count)]
    for j in range(0, k, panel):
        own, at = j // 8, j % 8
        row = [jnp.broadcast_to(blocks[own][at + a:at + a + 1, :], shape) for a in range(panel)]
        column = [
            [jnp.broadcast_to(blocks[i][:, j + a:j + a + 1], shape) for i in range(own, count)]
            for a in range(panel)
        ]
        corner = {
            (b, a): jnp.broadcast_to(column[a][0][at + b:at + b + 1, :], shape)
            for a in range(panel) for b in range(a, panel)
        }
        scaled = []
        for a in range(panel):
            pivot = corner[a, a]
            pivots[own] = jnp.where(sub == at + a, pivot, pivots[own])
            inverse = 1.0 / pivot
            scaled.append(row[a] * inverse)
            factor = {b: corner[b, a] * inverse for b in range(a + 1, panel)}
            for b in range(a + 1, panel):
                for c in range(b, panel):
                    corner[c, b] = corner[c, b] - factor[b] * corner[c, a]
            for b in range(a + 1, panel):
                row[b] = row[b] - factor[b] * row[a]
                column[b] = [y - factor[b] * x for x, y in zip(column[a], column[b])]
        for i in range(own, count):
            change = column[0][i - own] * scaled[0]
            for a in range(1, panel):
                change = change + column[a][i - own] * scaled[a]
            value = blocks[i] - change
            if i == own:
                value = jnp.where(sub >= at + panel, value, blocks[i])
                for a in range(panel):
                    value = jnp.where(sub == at + a, row[a], value)
            blocks[i] = value
    done = [blocks[i] * (1.0 / jnp.sqrt(pivots[i])) for i in range(count)]
    return jnp.concatenate(done, axis=0)[:, k:]


def pack(x):
    k = x.shape[0]
    return jnp.concatenate([x[:k // 2], x[k // 2:]], axis=1)


def unpack(x):
    k = x.shape[1] // 2
    return jnp.concatenate([x[:, :k], x[:, k:]], axis=0)


def flip(x, mask):
    result, bit = x, 1
    while bit <= mask:
        if mask & bit:
            result = result + bit - 2 * bit * lax.rem(lax.div(x, bit), 2)
        bit *= 2
    return result


def kernel(
    n, m, points, s_hbm, land_hbm, pen_hbm, v_hbm, out_ref, ray_ref,
    land_ref, pen_ref, s_full, s_high, s_mid, field0, field1, field2, lap_ref, v_split,
    cbuf, rs, zr, fin, g_in, gr, gz, g_out, plane, edge, halo, sides,
    c_sem, s_sem, v_sem, rs_s, rs_r, z_s, z_r, ag_s, ag_r, gr_s, gr_r, gz_s, gz_r, ga_s, ga_r,
    pl_s, pl_r, h_s, h_r,
):
    lat = lax.axis_index("lat")
    lon = lax.axis_index("lon")
    t_count, a_count, b_count = s_hbm.shape
    k = v_hbm.shape[0]
    fields = (field0, field1, field2)
    blocks = t_count // b_count
    pairs = blocks // 2
    per = n // blocks
    shard = k // per
    halves = 2
    part_rows = shard // halves
    wide = 2 * b_count
    gram_rows = k // blocks
    edge_groups = b_count // (2 * a_count)
    edge_rows = k // edge_groups
    inverse_points = 1.0 / points
    pending = []
    own_block = lax.div(lat, per)
    own_piece = lax.rem(lat, per)
    even = lax.rem(own_block, 2) == 0
    chip = lax.div(own_block, 2)

    def part(a):
        return pl.ds(a * b_count, b_count)

    def pair_rows(i):
        return pl.ds(pl.multiple_of(flip(chip, i) * wide, wide), wide)

    def piece_rows(piece, h=None):
        if h is None:
            return pl.ds(pl.multiple_of(piece * shard, shard), shard)
        return pl.ds(pl.multiple_of(piece * shard + h * part_rows, part_rows), part_rows)

    order = list(reversed(range(pairs)))
    groups = [order[g:g + 2] for g in range(0, pairs, 2)]
    land_copy = pltpu.make_async_copy(land_hbm, land_ref, c_sem.at[0])
    pen_copy = pltpu.make_async_copy(pen_hbm, pen_ref, c_sem.at[1])
    v_copies = [
        pltpu.make_async_copy(v_hbm.at[:, a, :], lap_ref.at[:, part(a)], v_sem.at[a])
        for a in range(a_count)
    ]
    s_copies = [
        [
            pltpu.make_async_copy(
                s_hbm.at[pair_rows(i), a, :], s_full.at[pair_rows(i), part(a)], s_sem.at[i, a]
            )
            for a in range(a_count)
        ]
        for i in range(pairs)
    ]
    land_copy.start()
    for copy in v_copies:
        copy.start()
    for i in reversed(range(pairs)):
        for copy in s_copies[i]:
            copy.start()
    pen_copy.start()

    barrier = pltpu.get_barrier_semaphore()
    for d in range(1, n):
        pl.semaphore_signal(barrier, inc=1, device_id=(flip(lat, d), lon), device_id_type=MESH)
    for e in range(1, m):
        pl.semaphore_signal(barrier, inc=1, device_id=(lat, flip(lon, e)), device_id_type=MESH)

    def send(src, dst, s_s, s_r, where):
        copy = pltpu.make_async_remote_copy(
            src_ref=src, dst_ref=dst, send_sem=s_s, recv_sem=s_r,
            device_id=where, device_id_type=MESH,
        )
        copy.start()
        pending.append(copy)
        return copy

    def to_lat(d):
        return (flip(lat, d), lon)

    def to_lon(e):
        return (lat, flip(lon, e))

    lane = lax.broadcasted_iota(jnp.int32, (k, b_count), 1)

    def mask_row(a):
        return land_ref[a:a + 1, :].astype(F32)

    def start_halo(r):
        x = fields[r]
        packed = jnp.zeros((k, b_count), F32)
        for a in range(a_count):
            block = x[:, a * b_count:(a + 1) * b_count]
            low = block if a == 0 else pltpu.roll(block, a, axis=1)
            high = pltpu.roll(block, a_count + a + 1, axis=1)
            packed = jnp.where(lane == a, low, packed)
            packed = jnp.where(lane == a_count + a, high, packed)
        narrow = packed[:edge_rows]
        for q in range(1, edge_groups):
            rows = packed[q * edge_rows:(q + 1) * edge_rows]
            narrow = narrow + pltpu.roll(rows, q * 2 * a_count, axis=1)
        edge[r] = narrow
        up, down = (lax.rem(lat + 1, n), lon), (lax.rem(lat + n - 1, n), lon)
        right, left = (lat, lax.rem(lon + 1, m)), (lat, lax.rem(lon + m - 1, m))
        return [
            send(x.at[:, part(a_count - 1)], halo.at[r, 0], h_s.at[r, 0], h_r.at[r, 0], up),
            send(x.at[:, part(0)], halo.at[r, 1], h_s.at[r, 1], h_r.at[r, 1], down),
            send(edge.at[r], sides.at[r, 0], h_s.at[r, 2], h_r.at[r, 2], right),
            send(edge.at[r], sides.at[r, 1], h_s.at[r, 3], h_r.at[r, 3], left),
        ]

    def widen(x):
        return jnp.concatenate(
            [x] + [
                pltpu.roll(x, b_count - q * 2 * a_count, axis=1) for q in range(1, edge_groups)
            ], axis=0,
        )

    def laplacian(r, copies):
        for copy in copies:
            copy.wait_recv()
        x = fields[r]
        above = jnp.where(lat > 0, halo[r, 0], 0.0)
        below = jnp.where(lat < n - 1, halo[r, 1], 0.0)
        west = jnp.where(lon > 0, widen(sides[r, 0]), 0.0)
        east = jnp.where(lon < m - 1, widen(sides[r, 1]), 0.0)
        for a in range(a_count):
            block = x[:, a * b_count:(a + 1) * b_count]
            up = above if a == 0 else x[:, (a - 1) * b_count:a * b_count]
            down = below if a == a_count - 1 else x[:, (a + 1) * b_count:(a + 2) * b_count]
            left = jnp.where(
                lane == 0, pltpu.roll(west, b_count - a_count - a, axis=1),
                pltpu.roll(block, 1, axis=1),
            )
            right = jnp.where(
                lane == b_count - 1, pltpu.roll(east, b_count - 1 - a, axis=1),
                pltpu.roll(block, b_count - 1, axis=1),
            )
            total = (down + up + right + left) - 4.0 * block
            lap_ref[:, a * b_count:(a + 1) * b_count] = total * pen_ref[a:a + 1, :]

    def store_field(r, a, value):
        x = value * mask_row(a)
        at = slice(a * b_count, (a + 1) * b_count)
        fields[r][:, at] = x
        v_split[:, at] = split3(x)

    def project_pair(r, i):
        rows = pair_rows(i)
        if r == 0:
            for copy in s_copies[i]:
                copy.wait()
            high, mid = split(s_full[rows, :])
            s_high[rows, :] = high
            s_mid[rows, :] = mid
        else:
            high, mid = s_high[rows, :], s_mid[rows, :]
        both = dot_low(v_split[:2 * k, :], high, NT)
        rest = dot_low(v_split[:k, :], mid, NT)
        value = both[:k] + (both[k:] + rest)
        low, up = value[:, :b_count], value[:, b_count:]
        cbuf[r, 2 * i] = jnp.where(even, low, up)
        cbuf[r, 2 * i + 1] = jnp.where(even, up, low)

    def send_pair(r, i, copies):
        for e in (1, 0):
            for q in range(per):
                d = (2 * i + e) * per + q
                if d:
                    rows = piece_rows(lax.rem(flip(lat, d), per))
                    copies[d] = send(
                        cbuf.at[r, 2 * i + e, rows], rs.at[r, d],
                        rs_s.at[r, d], rs_r.at[r, d], to_lat(d),
                    )

    def project(r):
        copies = {}
        for group in groups:
            for i in group:
                project_pair(r, i)
            for i in group:
                send_pair(r, i, copies)
        return copies

    def finish_scatter(r, copies):
        for d in sorted(copies, reverse=True):
            copies[d].wait_recv()
        result = []
        for h in range(halves):
            total = cbuf[r, 0, piece_rows(own_piece, h), :]
            at = slice(h * part_rows, (h + 1) * part_rows)
            for d in range(1, n):
                total = total + rs[r, d, at, :]
            zr[r, lon, at, :] = total
            result.append([
                send(
                    zr.at[r, lon, pl.ds(h * part_rows, part_rows)],
                    zr.at[r, lon, pl.ds(h * part_rows, part_rows)],
                    z_s.at[r, h, e], z_r.at[r, h, e], to_lon(e),
                )
                for e in reversed(range(1, m))
            ])
        return result

    def finish_lon(r, h, copies):
        for copy in copies[h]:
            copy.wait_recv()
        at = slice(h * part_rows, (h + 1) * part_rows)
        total = zr[r, 0, at, :]
        for e in range(1, m):
            total = total + zr[r, e, at, :]
        fin[r, 0, piece_rows(own_piece, h), :] = total

    def start_gather(r, copies):
        gathers = {}
        for h in range(halves):
            finish_lon(r, h, copies)
            rows = piece_rows(own_piece, h)
            for d in reversed(range(1, n)):
                gathers[h, d] = send(
                    fin.at[r, 0, rows], fin.at[r, d // per, rows],
                    ag_s.at[r, h, d], ag_r.at[r, h, d], to_lat(d),
                )
        return gathers

    def wait_block(block, copies):
        for q in range(per):
            d = block * per + q
            for h in range(halves):
                if d:
                    copies[h, d].wait_recv()

    def gram_piece(block):
        return pl.ds(pl.multiple_of(block * gram_rows, gram_rows), gram_rows)

    def start_gram(r, value):
        g_in[r] = jnp.concatenate([value, value], axis=1)
        gr[r, lat] = g_in[r, gram_piece(own_block), :]
        return [
            send(
                g_in.at[r, gram_piece(flip(own_block, d // per))], gr.at[r, lat],
                gr_s.at[r, d], gr_r.at[r, d], to_lat(d),
            )
            for d in reversed(range(1, n))
        ]

    def middle_gram(r, copies):
        for copy in copies:
            copy.wait_recv()
        total = gr[r, 0]
        for d in range(1, n):
            total = total + gr[r, d]
        gz[r, lon] = total
        return [
            send(gz.at[r, lon], gz.at[r, lon], gz_s.at[r, e], gz_r.at[r, e], to_lon(e))
            for e in reversed(range(1, m))
        ]

    def sum_gram(r, copies):
        for copy in copies:
            copy.wait_recv()
        total = gz[r, 0]
        for e in range(1, m):
            total = total + gz[r, e]
        return total

    def spread_gram(r, copies):
        g_out[r, gram_piece(own_block), :] = sum_gram(r, copies)
        rows = gram_piece(own_block)
        return [
            send(
                g_out.at[r, rows], g_out.at[r, rows],
                ga_s.at[r, block], ga_r.at[r, block], to_lat(block * per),
            )
            for block in reversed(range(1, blocks))
        ]

    def finish_gram(r, copies):
        for copy in copies:
            copy.wait_recv()
        return g_out[r, :, :k]

    def start_plane(value):
        plane[lat] = value
        return [
            send(plane.at[lat], plane.at[lat], pl_s.at[d], pl_r.at[d], to_lat(d))
            for d in reversed(range(1, n))
        ]

    def finish_plane(copies):
        for copy in copies:
            copy.wait_recv()
        total = plane[0]
        for d in range(1, n):
            total = total + plane[d]
        return total

    def expand(r, copies, parts=None):
        for i in range(pairs):
            for e in range(2):
                wait_block(2 * i + e, copies)
            near, far = fin[r - 1, 2 * i], fin[r - 1, 2 * i + 1]
            coeffs = jnp.concatenate(
                [jnp.where(even, near, far), jnp.where(even, far, near)], axis=1
            )
            high, mid = split(coeffs * inverse_points)
            stacked = jnp.concatenate([high, mid], axis=0)
            rows = pair_rows(i)
            for block in range(a_count // 2):
                at = slice(block * wide, (block + 1) * wide)
                both = dot_low(stacked, s_high[rows, at], NN)
                rest = dot_low(high, s_mid[rows, at], NN)
                value = lap_ref[:, at] + (both[:k] + (both[k:] + rest))
                if i < pairs - 1:
                    lap_ref[:, at] = value
                else:
                    if parts is not None:
                        value = times(parts, split3(value))
                    store_field(r, 2 * block, value[:, :b_count])
                    store_field(r, 2 * block + 1, value[:, b_count:])

    def gram():
        return products(v_split[...], v_split[...]) * inverse_points

    land_copy.wait()
    for a in range(a_count):
        v_copies[a].wait()
        store_field(0, a, lap_ref[:, a * b_count:(a + 1) * b_count])
    for i in groups[0]:
        project_pair(0, i)
    pl.semaphore_wait(barrier, n + m - 2)
    copies = {}
    for i in groups[0]:
        send_pair(0, i, copies)
    for group in groups[1:]:
        for i in group:
            project_pair(0, i)
        for i in group:
            send_pair(0, i, copies)
    halo_copies = start_halo(0)
    pen_copy.wait()
    copies = finish_scatter(0, copies)
    laplacian(0, halo_copies)
    copies = start_gather(0, copies)
    expand(1, copies)

    gram_copies = start_gram(0, gram())
    copies = project(1)
    halo_copies = start_halo(1)
    gram_copies = middle_gram(0, gram_copies)
    copies = finish_scatter(1, copies)
    gram_copies = spread_gram(0, gram_copies)
    laplacian(1, halo_copies)
    copies = start_gather(1, copies)
    parts = factor_parts(inverse_factor(finish_gram(0, gram_copies)))
    expand(2, copies, parts)

    gram_copies = start_gram(1, gram())
    halo_copies = start_halo(2)
    copies = project(2)
    gram_copies = middle_gram(1, gram_copies)
    laplacian(2, halo_copies)
    rough_copies = start_gram(2, products(v_split[...], split3(lap_ref[...])))
    copies = finish_scatter(2, copies)
    gram_copies = spread_gram(1, gram_copies)
    rough_copies = middle_gram(2, rough_copies)
    inverse = inverse_factor(finish_gram(1, gram_copies))
    rows = gram_piece(own_block)
    if per == 1:
        for h in range(halves):
            finish_lon(2, h, copies)
        coeffs = split3(fin[2, 0])
        middle = products(coeffs, coeffs) * inverse_points
        g_out[2] = jnp.concatenate([middle, middle], axis=1)
    else:
        g_out[2] = jnp.zeros((k, b_count), F32)
        copies = start_gather(2, copies)
    rough = jnp.where(own_piece == 0, sum_gram(2, rough_copies), 0.0)
    g_out[2, rows, :] = g_out[2, rows, :] + rough
    plane_copies = start_plane(pack(g_out[2, :, :k]))
    parts = factor_parts(inverse)
    for block in range(a_count // 2):
        at = slice(block * wide, (block + 1) * wide)
        out_ref[:, at] = times(parts, v_split[:, at])
    middle = unpack(finish_plane(plane_copies))
    if per > 1:
        for block in range(blocks):
            wait_block(block, copies)
        coeffs = split3(jnp.concatenate(
            [fin[2, flip(own_block, block)] for block in range(blocks)], axis=1
        ))
        middle = middle + products(coeffs, coeffs) * inverse_points
    ray_ref[...] = dot_full(dot_full(inverse, middle, NN), inverse, NT) * inverse_points
    for copy in pending:
        copy.wait_send()


def write_out(x_ref, ray_ref, out_hbm, ray_hbm, sems):
    a_count, b_count = out_hbm.shape[1:]
    copies = [pltpu.make_async_copy(ray_ref, ray_hbm, sems.at[a_count])]
    for a in range(a_count):
        at = pl.ds(a * b_count, b_count)
        copies.append(pltpu.make_async_copy(x_ref.at[:, at], out_hbm.at[:, a, :], sems.at[a]))
    for copy in copies:
        copy.start()
    for copy in copies:
        copy.wait()


def local(snapshots, land_sea, penalty, initial_basis):
    n, m = lax.axis_size("lat"), lax.axis_size("lon")
    t, a, b = snapshots.shape
    k = initial_basis.shape[0]
    points = float(a * b * n * m)
    p = a * b
    blocks = t // b
    shard = blocks * k // n
    sem = pltpu.SemaphoreType.DMA
    vmem = pltpu.VMEM
    any_spec = pl.BlockSpec(memory_space=pl.ANY)
    vmem_spec = pl.BlockSpec(memory_space=pltpu.VMEM)
    out, ray = pl.pallas_call(
        functools.partial(kernel, n, m, points),
        out_shape=(vmem((k, p), F32), vmem((k, k), F32)),
        in_specs=[any_spec, any_spec, any_spec, any_spec],
        out_specs=(vmem_spec, vmem_spec),
        scratch_shapes=[
            vmem((a, b), jnp.int32), vmem((a, b), F32),
            vmem((t, p), F32), vmem((t, p), BF16), vmem((t, p), BF16),
            vmem((k, p), F32), vmem((k, p), F32), vmem((k, p), F32),
            vmem((k, p), F32), vmem((3 * k, p), BF16),
            vmem((3, blocks, k, b), F32), vmem((3, n, shard, b), F32), vmem((3, m, shard, b), F32),
            vmem((3, blocks, k, b), F32), vmem((3, k, b), F32), vmem((3, n, k // blocks, b), F32),
            vmem((3, m, k // blocks, b), F32), vmem((3, k, b), F32), vmem((n, k // 2, b), F32),
            vmem((3, 2 * a * k // b, b), F32), vmem((3, 2, k, b), F32),
            vmem((3, 2, 2 * a * k // b, b), F32),
            sem((2,)), sem((blocks // 2, a)), sem((a,)),
            sem((3, n)), sem((3, n)), sem((3, 2, m)), sem((3, 2, m)), sem((3, 2, n)), sem((3, 2, n)),
            sem((3, n)), sem((3, n)), sem((3, m)), sem((3, m)), sem((3, blocks)), sem((3, blocks)),
            sem((n,)), sem((n,)), sem((3, 4)), sem((3, 4)),
        ],
        compiler_params=pltpu.CompilerParams(
            collective_id=0, has_side_effects=True, vmem_limit_bytes=60 * 1024 * 1024
        ),
        name="power_steps",
    )(snapshots, land_sea, penalty, initial_basis)
    return pl.pallas_call(
        write_out,
        out_shape=(jax.ShapeDtypeStruct((k, a, b), F32), jax.ShapeDtypeStruct((k, k), F32)),
        in_specs=[vmem_spec, vmem_spec],
        out_specs=(any_spec, any_spec),
        scratch_shapes=[sem((a + 1,))],
        name="write_out",
    )(
        pltpu.with_memory_space_constraint(out, pltpu.VMEM),
        pltpu.with_memory_space_constraint(ray, pltpu.VMEM),
    )


def solution(mesh):
    in_specs = (P(None, "lat", "lon"), P("lat", "lon"), P("lat", "lon"), P(None, "lat", "lon"))
    out_specs = (P(None, "lat", "lon"), P())
    return jax.shard_map(local, mesh=mesh, in_specs=in_specs, out_specs=out_specs, check_vma=False)
```

```python
import functools

import jax
import jax.numpy as jnp
from jax import lax
from jax.experimental import pallas as pl
from jax.experimental.pallas import tpu as pltpu
from jax.sharding import PartitionSpec as P

STEPS = 2
MESH = pl.DeviceIdType.MESH
F32 = jnp.float32
BF16 = jnp.bfloat16
NT = (((1,), (1,)), ((), ()))
NN = (((1,), (0,)), ((), ()))


def dot_low(a, b, dims):
    return lax.dot_general(a, b, dims, preferred_element_type=F32)


def split(x):
    high = x.astype(BF16)
    return high, (x - high.astype(F32)).astype(BF16)


def split3(x):
    high = x.astype(BF16)
    rest = x - high.astype(F32)
    mid = rest.astype(BF16)
    return jnp.concatenate([high, mid, (rest - mid.astype(F32)).astype(BF16)], axis=0)


def fold_rows(x, k):
    return x[:k] + (x[k:2 * k] + x[2 * k:])


def products(left, right):
    k = left.shape[0] // 3
    x = fold_rows(dot_low(left, right, NT), k)
    return x[:, :k] + (x[:, k:2 * k] + x[:, 2 * k:])


def factor_parts(inverse):
    k = inverse.shape[0]
    parts = split3(inverse)
    return jnp.concatenate([parts, parts, parts], axis=1)


def times(parts, right):
    return fold_rows(dot_low(parts, right, NN), parts.shape[0] // 3)


def inverse_factor(gram):
    k = gram.shape[0]
    panel = 4
    rows = lax.broadcasted_iota(jnp.int32, (k, k), 0)
    cols = lax.broadcasted_iota(jnp.int32, (k, k), 1)
    eye = jnp.where(rows == cols, 1.0, 0.0).astype(F32)
    work = jnp.concatenate([gram, eye], axis=1)
    count = k // 8
    shape = (8, 2 * k)
    blocks = [work[8 * i:8 * i + 8] for i in range(count)]
    sub = lax.broadcasted_iota(jnp.int32, shape, 0)
    pivots = [jnp.zeros(shape, F32) for _ in range(count)]
    for j in range(0, k, panel):
        own, at = j // 8, j % 8
        row = [jnp.broadcast_to(blocks[own][at + a:at + a + 1, :], shape) for a in range(panel)]
        column = [
            [jnp.broadcast_to(blocks[i][:, j + a:j + a + 1], shape) for i in range(own, count)]
            for a in range(panel)
        ]
        corner = {
            (b, a): jnp.broadcast_to(column[a][0][at + b:at + b + 1, :], shape)
            for a in range(panel) for b in range(a, panel)
        }
        scaled = []
        for a in range(panel):
            pivot = corner[a, a]
            pivots[own] = jnp.where(sub == at + a, pivot, pivots[own])
            inverse = 1.0 / pivot
            scaled.append(row[a] * inverse)
            factor = {b: corner[b, a] * inverse for b in range(a + 1, panel)}
            for b in range(a + 1, panel):
                for c in range(b, panel):
                    corner[c, b] = corner[c, b] - factor[b] * corner[c, a]
            for b in range(a + 1, panel):
                row[b] = row[b] - factor[b] * row[a]
                column[b] = [y - factor[b] * x for x, y in zip(column[a], column[b])]
        for i in range(own, count):
            change = column[0][i - own] * scaled[0]
            for a in range(1, panel):
                change = change + column[a][i - own] * scaled[a]
            value = blocks[i] - change
            if i == own:
                value = jnp.where(sub >= at + panel, value, blocks[i])
                for a in range(panel):
                    value = jnp.where(sub == at + a, row[a], value)
            blocks[i] = value
    done = [blocks[i] * (1.0 / jnp.sqrt(pivots[i])) for i in range(count)]
    return jnp.concatenate(done, axis=0)[:, k:]


def pack(x):
    k = x.shape[0]
    return jnp.concatenate([x[:k // 2], x[k // 2:]], axis=1)


def unpack(x):
    k = x.shape[1] // 2
    return jnp.concatenate([x[:, :k], x[:, k:]], axis=0)


def flip(x, mask):
    result, bit = x, 1
    while bit <= mask:
        if mask & bit:
            result = result + bit - 2 * bit * lax.rem(lax.div(x, bit), 2)
        bit *= 2
    return result


def kernel(
    n, m, points, s_hbm, land_hbm, pen_hbm, v_hbm, out_ref, ray_ref,
    land_ref, pen_ref, s_full, s_high, s_mid, t_high, t_mid, field0, field1, field2, lap_ref, v_split,
    cbuf, rs, zr, fin, g_in, gr, gz, g_out, plane, edge, halo, sides,
    c_sem, s_sem, v_sem, rs_s, rs_r, z_s, z_r, ag_s, ag_r, gr_s, gr_r, gz_s, gz_r, ga_s, ga_r,
    pl_s, pl_r, h_s, h_r,
):
    lat = lax.axis_index("lat")
    lon = lax.axis_index("lon")
    t_count, a_count, b_count = s_hbm.shape
    k = v_hbm.shape[0]
    fields = (field0, field1, field2)
    blocks = t_count // b_count
    pairs = blocks // 2
    per = n // blocks
    shard = k // per
    halves = 2
    part_rows = shard // halves
    wide = 2 * b_count
    gram_rows = k // blocks
    edge_groups = b_count // (2 * a_count)
    edge_rows = k // edge_groups
    inverse_points = 1.0 / points
    pending = []
    own_block = lax.div(lat, per)
    own_piece = lax.rem(lat, per)
    even = lax.rem(own_block, 2) == 0
    chip = lax.div(own_block, 2)

    def part(a):
        return pl.ds(a * b_count, b_count)

    def pair_rows(i):
        return pl.ds(pl.multiple_of(flip(chip, i) * wide, wide), wide)

    def piece_rows(piece, h=None):
        if h is None:
            return pl.ds(pl.multiple_of(piece * shard, shard), shard)
        return pl.ds(pl.multiple_of(piece * shard + h * part_rows, part_rows), part_rows)

    half_rows = a_count // 2
    order = list(reversed(range(pairs)))
    groups = [order[g:g + 2] for g in range(0, pairs, 2)]
    land_copy = pltpu.make_async_copy(land_hbm, land_ref, c_sem.at[0])
    pen_copy = pltpu.make_async_copy(pen_hbm, pen_ref, c_sem.at[1])
    v_copies = [
        pltpu.make_async_copy(v_hbm.at[:, a, :], lap_ref.at[:, part(a)], v_sem.at[a])
        for a in range(a_count)
    ]
    s_copies = [
        [
            pltpu.make_async_copy(
                s_hbm.at[pair_rows(i), a, :], s_full.at[pair_rows(i), part(a)], s_sem.at[i, a]
            )
            for a in range(a_count)
        ]
        for i in range(pairs)
    ]
    land_copy.start()
    for copy in v_copies:
        copy.start()
    for group in groups:
        for h in range(2):
            for i in group:
                for copy in s_copies[i][h * half_rows:(h + 1) * half_rows]:
                    copy.start()
    pen_copy.start()

    barrier = pltpu.get_barrier_semaphore()
    for d in range(1, n):
        pl.semaphore_signal(barrier, inc=1, device_id=(flip(lat, d), lon), device_id_type=MESH)
    for e in range(1, m):
        pl.semaphore_signal(barrier, inc=1, device_id=(lat, flip(lon, e)), device_id_type=MESH)

    def send(src, dst, s_s, s_r, where):
        copy = pltpu.make_async_remote_copy(
            src_ref=src, dst_ref=dst, send_sem=s_s, recv_sem=s_r,
            device_id=where, device_id_type=MESH,
        )
        copy.start()
        pending.append(copy)
        return copy

    def to_lat(d):
        return (flip(lat, d), lon)

    def to_lon(e):
        return (lat, flip(lon, e))

    lane = lax.broadcasted_iota(jnp.int32, (k, b_count), 1)

    def mask_row(a):
        return land_ref[a:a + 1, :].astype(F32)

    def start_halo(r):
        x = fields[r]
        packed = jnp.zeros((k, b_count), F32)
        for a in range(a_count):
            block = x[:, a * b_count:(a + 1) * b_count]
            low = block if a == 0 else pltpu.roll(block, a, axis=1)
            high = pltpu.roll(block, a_count + a + 1, axis=1)
            packed = jnp.where(lane == a, low, packed)
            packed = jnp.where(lane == a_count + a, high, packed)
        narrow = packed[:edge_rows]
        for q in range(1, edge_groups):
            rows = packed[q * edge_rows:(q + 1) * edge_rows]
            narrow = narrow + pltpu.roll(rows, q * 2 * a_count, axis=1)
        edge[r] = narrow
        up, down = (lax.rem(lat + 1, n), lon), (lax.rem(lat + n - 1, n), lon)
        right, left = (lat, lax.rem(lon + 1, m)), (lat, lax.rem(lon + m - 1, m))
        return [
            send(x.at[:, part(a_count - 1)], halo.at[r, 0], h_s.at[r, 0], h_r.at[r, 0], up),
            send(x.at[:, part(0)], halo.at[r, 1], h_s.at[r, 1], h_r.at[r, 1], down),
            send(edge.at[r], sides.at[r, 0], h_s.at[r, 2], h_r.at[r, 2], right),
            send(edge.at[r], sides.at[r, 1], h_s.at[r, 3], h_r.at[r, 3], left),
        ]

    def widen(x):
        return jnp.concatenate(
            [x] + [
                pltpu.roll(x, b_count - q * 2 * a_count, axis=1) for q in range(1, edge_groups)
            ], axis=0,
        )

    def laplacian(r, copies):
        for copy in copies:
            copy.wait_recv()
        x = fields[r]
        above = jnp.where(lat > 0, halo[r, 0], 0.0)
        below = jnp.where(lat < n - 1, halo[r, 1], 0.0)
        west = jnp.where(lon > 0, widen(sides[r, 0]), 0.0)
        east = jnp.where(lon < m - 1, widen(sides[r, 1]), 0.0)
        for a in range(a_count):
            block = x[:, a * b_count:(a + 1) * b_count]
            up = above if a == 0 else x[:, (a - 1) * b_count:a * b_count]
            down = below if a == a_count - 1 else x[:, (a + 1) * b_count:(a + 2) * b_count]
            left = jnp.where(
                lane == 0, pltpu.roll(west, b_count - a_count - a, axis=1),
                pltpu.roll(block, 1, axis=1),
            )
            right = jnp.where(
                lane == b_count - 1, pltpu.roll(east, b_count - 1 - a, axis=1),
                pltpu.roll(block, b_count - 1, axis=1),
            )
            total = (down + up + right + left) - 4.0 * block
            lap_ref[:, a * b_count:(a + 1) * b_count] = total * pen_ref[a:a + 1, :]

    def store_field(r, a, value):
        x = value * mask_row(a)
        at = slice(a * b_count, (a + 1) * b_count)
        fields[r][:, at] = x
        v_split[:, at] = split3(x)

    def store_pair(r, i, both, rest):
        value = both[:k] + (both[k:] + rest)
        low, up = value[:, :b_count], value[:, b_count:]
        cbuf[r, 2 * i] = jnp.where(even, low, up)
        cbuf[r, 2 * i + 1] = jnp.where(even, up, low)

    def project_first(group):
        sums = {}
        for h in range(2):
            at = slice(h * half_rows * b_count, (h + 1) * half_rows * b_count)
            for i in group:
                for copy in s_copies[i][h * half_rows:(h + 1) * half_rows]:
                    copy.wait()
            for i in group:
                rows = pair_rows(i)
                high, mid = split(s_full[rows, at])
                s_high[rows, at] = high
                s_mid[rows, at] = mid
                both = dot_low(v_split[:2 * k, at], high, NT)
                rest = dot_low(v_split[:k, at], mid, NT)
                if h:
                    store_pair(0, i, sums[i][0] + both, sums[i][1] + rest)
                else:
                    sums[i] = both, rest

    def project_pair(r, i):
        rows = pair_rows(i)
        both = dot_low(v_split[:2 * k, :], t_high[:, rows], NN)
        rest = dot_low(v_split[:k, :], t_mid[:, rows], NN)
        store_pair(r, i, both, rest)

    def turn(source, target):
        for i in range(pairs):
            rows = slice(i * wide, (i + 1) * wide)
            for block in range(a_count // 2):
                at = slice(block * wide, (block + 1) * wide)
                target[at, rows] = source[rows, at].T

    def send_pair(r, i, copies):
        for e in (1, 0):
            for q in range(per):
                d = (2 * i + e) * per + q
                if d:
                    rows = piece_rows(lax.rem(flip(lat, d), per))
                    copies[d] = send(
                        cbuf.at[r, 2 * i + e, rows], rs.at[r, d],
                        rs_s.at[r, d], rs_r.at[r, d], to_lat(d),
                    )

    def project(r):
        copies = {}
        for group in groups:
            for i in group:
                project_pair(r, i)
            for i in group:
                send_pair(r, i, copies)
        return copies

    def finish_scatter(r, copies):
        for d in sorted(copies, reverse=True):
            copies[d].wait_recv()
        result = []
        for h in range(halves):
            total = cbuf[r, 0, piece_rows(own_piece, h), :]
            at = slice(h * part_rows, (h + 1) * part_rows)
            for d in range(1, n):
                total = total + rs[r, d, at, :]
            zr[r, lon, at, :] = total
            result.append([
                send(
                    zr.at[r, lon, pl.ds(h * part_rows, part_rows)],
                    zr.at[r, lon, pl.ds(h * part_rows, part_rows)],
                    z_s.at[r, h, e], z_r.at[r, h, e], to_lon(e),
                )
                for e in reversed(range(1, m))
            ])
        return result

    def finish_lon(r, h, copies):
        for copy in copies[h]:
            copy.wait_recv()
        at = slice(h * part_rows, (h + 1) * part_rows)
        total = zr[r, 0, at, :]
        for e in range(1, m):
            total = total + zr[r, e, at, :]
        fin[r, 0, piece_rows(own_piece, h), :] = total

    def start_gather(r, copies):
        gathers = {}
        for h in range(halves):
            finish_lon(r, h, copies)
            rows = piece_rows(own_piece, h)
            for d in reversed(range(1, n)):
                gathers[h, d] = send(
                    fin.at[r, 0, rows], fin.at[r, d // per, rows],
                    ag_s.at[r, h, d], ag_r.at[r, h, d], to_lat(d),
                )
        return gathers

    def wait_block(block, copies):
        for q in range(per):
            d = block * per + q
            for h in range(halves):
                if d:
                    copies[h, d].wait_recv()

    def gram_piece(block):
        return pl.ds(pl.multiple_of(block * gram_rows, gram_rows), gram_rows)

    def start_gram(r, value):
        g_in[r] = jnp.concatenate([value, value], axis=1)
        gr[r, lat] = g_in[r, gram_piece(own_block), :]
        return [
            send(
                g_in.at[r, gram_piece(flip(own_block, d // per))], gr.at[r, lat],
                gr_s.at[r, d], gr_r.at[r, d], to_lat(d),
            )
            for d in reversed(range(1, n))
        ]

    def middle_gram(r, copies):
        for copy in copies:
            copy.wait_recv()
        total = gr[r, 0]
        for d in range(1, n):
            total = total + gr[r, d]
        gz[r, lon] = total
        return [
            send(gz.at[r, lon], gz.at[r, lon], gz_s.at[r, e], gz_r.at[r, e], to_lon(e))
            for e in reversed(range(1, m))
        ]

    def sum_gram(r, copies):
        for copy in copies:
            copy.wait_recv()
        total = gz[r, 0]
        for e in range(1, m):
            total = total + gz[r, e]
        return total

    def spread_gram(r, copies):
        g_out[r, gram_piece(own_block), :] = sum_gram(r, copies)
        rows = gram_piece(own_block)
        return [
            send(
                g_out.at[r, rows], g_out.at[r, rows],
                ga_s.at[r, block], ga_r.at[r, block], to_lat(block * per),
            )
            for block in reversed(range(1, blocks))
        ]

    def finish_gram(r, copies):
        for copy in copies:
            copy.wait_recv()
        return g_out[r, :, :k]

    def start_plane(value):
        plane[lat] = value
        return [
            send(plane.at[lat], plane.at[lat], pl_s.at[d], pl_r.at[d], to_lat(d))
            for d in reversed(range(1, n))
        ]

    def finish_plane(copies):
        for copy in copies:
            copy.wait_recv()
        total = plane[0]
        for d in range(1, n):
            total = total + plane[d]
        return total

    def expand_pair(r, i, copies, parts=None):
        for e in range(2):
            wait_block(2 * i + e, copies)
        near, far = fin[r - 1, 2 * i], fin[r - 1, 2 * i + 1]
        coeffs = jnp.concatenate(
            [jnp.where(even, near, far), jnp.where(even, far, near)], axis=1
        )
        high, mid = split(coeffs * inverse_points)
        stacked = jnp.concatenate([high, mid], axis=0)
        rows = pair_rows(i)
        for block in range(a_count // 2):
            at = slice(block * wide, (block + 1) * wide)
            both = dot_low(stacked, s_high[rows, at], NN)
            rest = dot_low(high, s_mid[rows, at], NN)
            value = lap_ref[:, at] + (both[:k] + (both[k:] + rest))
            if i < pairs - 1:
                lap_ref[:, at] = value
            else:
                if parts is not None:
                    value = times(parts, split3(value))
                store_field(r, 2 * block, value[:, :b_count])
                store_field(r, 2 * block + 1, value[:, b_count:])

    def gram():
        return products(v_split[...], v_split[...]) * inverse_points

    land_copy.wait()
    for a in range(a_count):
        v_copies[a].wait()
        store_field(0, a, lap_ref[:, a * b_count:(a + 1) * b_count])
    project_first(groups[0])
    pl.semaphore_wait(barrier, n + m - 2)
    copies = {}
    for i in groups[0]:
        send_pair(0, i, copies)
    for group in groups[1:]:
        project_first(group)
        for i in group:
            send_pair(0, i, copies)
    halo_copies = start_halo(0)
    pen_copy.wait()
    turn(s_high, t_high)
    copies = finish_scatter(0, copies)
    turn(s_mid, t_mid)
    laplacian(0, halo_copies)
    copies = start_gather(0, copies)
    for i in range(pairs):
        expand_pair(1, i, copies)

    gram_copies = start_gram(0, gram())
    copies = project(1)
    halo_copies = start_halo(1)
    gram_copies = middle_gram(0, gram_copies)
    copies = finish_scatter(1, copies)
    gram_copies = spread_gram(0, gram_copies)
    laplacian(1, halo_copies)
    copies = start_gather(1, copies)
    expand_pair(2, 0, copies)
    parts = factor_parts(inverse_factor(finish_gram(0, gram_copies)))
    for i in range(1, pairs):
        expand_pair(2, i, copies, parts)

    gram_copies = start_gram(1, gram())
    halo_copies = start_halo(2)
    copies = project(2)
    gram_copies = middle_gram(1, gram_copies)
    laplacian(2, halo_copies)
    rough_copies = start_gram(2, products(v_split[...], split3(lap_ref[...])))
    copies = finish_scatter(2, copies)
    gram_copies = spread_gram(1, gram_copies)
    rough_copies = middle_gram(2, rough_copies)
    rows = gram_piece(own_block)
    if per == 1:
        for h in range(halves):
            finish_lon(2, h, copies)
        coeffs = split3(fin[2, 0])
        middle = products(coeffs, coeffs) * inverse_points
        g_out[2] = jnp.concatenate([middle, middle], axis=1)
    else:
        g_out[2] = jnp.zeros((k, b_count), F32)
        copies = start_gather(2, copies)
    rough = jnp.where(own_piece == 0, sum_gram(2, rough_copies), 0.0)
    g_out[2, rows, :] = g_out[2, rows, :] + rough
    plane_copies = start_plane(pack(g_out[2, :, :k]))
    inverse = inverse_factor(finish_gram(1, gram_copies))
    parts = factor_parts(inverse)
    for block in range(a_count // 2):
        at = slice(block * wide, (block + 1) * wide)
        out_ref[:, at] = times(parts, v_split[:, at])
    middle = unpack(finish_plane(plane_copies))
    if per > 1:
        for block in range(blocks):
            wait_block(block, copies)
        coeffs = split3(jnp.concatenate(
            [fin[2, flip(own_block, block)] for block in range(blocks)], axis=1
        ))
        middle = middle + products(coeffs, coeffs) * inverse_points
    half = times(parts, split3(middle))
    ray_ref[...] = products(split3(half), split3(inverse)) * inverse_points
    for copy in pending:
        copy.wait_send()


def write_out(x_ref, ray_ref, out_hbm, ray_hbm, sems):
    a_count, b_count = out_hbm.shape[1:]
    copies = [pltpu.make_async_copy(ray_ref, ray_hbm, sems.at[a_count])]
    for a in range(a_count):
        at = pl.ds(a * b_count, b_count)
        copies.append(pltpu.make_async_copy(x_ref.at[:, at], out_hbm.at[:, a, :], sems.at[a]))
    for copy in copies:
        copy.start()
    for copy in copies:
        copy.wait()


def local(snapshots, land_sea, penalty, initial_basis):
    n, m = lax.axis_size("lat"), lax.axis_size("lon")
    t, a, b = snapshots.shape
    k = initial_basis.shape[0]
    points = float(a * b * n * m)
    p = a * b
    blocks = t // b
    shard = blocks * k // n
    sem = pltpu.SemaphoreType.DMA
    vmem = pltpu.VMEM
    any_spec = pl.BlockSpec(memory_space=pl.ANY)
    vmem_spec = pl.BlockSpec(memory_space=pltpu.VMEM)
    out, ray = pl.pallas_call(
        functools.partial(kernel, n, m, points),
        out_shape=(vmem((k, p), F32), vmem((k, k), F32)),
        in_specs=[any_spec, any_spec, any_spec, any_spec],
        out_specs=(vmem_spec, vmem_spec),
        scratch_shapes=[
            vmem((a, b), jnp.int32), vmem((a, b), F32),
            vmem((t, p), F32), vmem((t, p), BF16), vmem((t, p), BF16),
            vmem((p, t), BF16), vmem((p, t), BF16),
            vmem((k, p), F32), vmem((k, p), F32), vmem((k, p), F32),
            vmem((k, p), F32), vmem((3 * k, p), BF16),
            vmem((3, blocks, k, b), F32), vmem((3, n, shard, b), F32), vmem((3, m, shard, b), F32),
            vmem((3, blocks, k, b), F32), vmem((3, k, b), F32), vmem((3, n, k // blocks, b), F32),
            vmem((3, m, k // blocks, b), F32), vmem((3, k, b), F32), vmem((n, k // 2, b), F32),
            vmem((3, 2 * a * k // b, b), F32), vmem((3, 2, k, b), F32),
            vmem((3, 2, 2 * a * k // b, b), F32),
            sem((2,)), sem((blocks // 2, a)), sem((a,)),
            sem((3, n)), sem((3, n)), sem((3, 2, m)), sem((3, 2, m)), sem((3, 2, n)), sem((3, 2, n)),
            sem((3, n)), sem((3, n)), sem((3, m)), sem((3, m)), sem((3, blocks)), sem((3, blocks)),
            sem((n,)), sem((n,)), sem((3, 4)), sem((3, 4)),
        ],
        compiler_params=pltpu.CompilerParams(
            collective_id=0, has_side_effects=True, vmem_limit_bytes=60 * 1024 * 1024
        ),
        name="power_steps",
    )(snapshots, land_sea, penalty, initial_basis)
    return pl.pallas_call(
        write_out,
        out_shape=(jax.ShapeDtypeStruct((k, a, b), F32), jax.ShapeDtypeStruct((k, k), F32)),
        in_specs=[vmem_spec, vmem_spec],
        out_specs=(any_spec, any_spec),
        scratch_shapes=[sem((a + 1,))],
        name="write_out",
    )(
        pltpu.with_memory_space_constraint(out, pltpu.VMEM),
        pltpu.with_memory_space_constraint(ray, pltpu.VMEM),
    )


def solution(mesh):
    in_specs = (P(None, "lat", "lon"), P("lat", "lon"), P("lat", "lon"), P(None, "lat", "lon"))
    out_specs = (P(None, "lat", "lon"), P())
    return jax.shard_map(local, mesh=mesh, in_specs=in_specs, out_specs=out_specs, check_vma=False)
```

```python
import functools

import jax
import jax.numpy as jnp
from jax import lax
from jax.experimental import pallas as pl
from jax.experimental.pallas import tpu as pltpu
from jax.sharding import PartitionSpec as P

STEPS = 2
MESH = pl.DeviceIdType.MESH
F32 = jnp.float32
BF16 = jnp.bfloat16
NT = (((1,), (1,)), ((), ()))
NN = (((1,), (0,)), ((), ()))


def dot_low(a, b, dims):
    return lax.dot_general(a, b, dims, preferred_element_type=F32)


def split(x):
    high = x.astype(BF16)
    return high, (x - high.astype(F32)).astype(BF16)


def split3(x):
    high = x.astype(BF16)
    rest = x - high.astype(F32)
    mid = rest.astype(BF16)
    return jnp.concatenate([high, mid, (rest - mid.astype(F32)).astype(BF16)], axis=0)


def fold_rows(x, k):
    return x[:k] + (x[k:2 * k] + x[2 * k:])


def products(left, right):
    k = left.shape[0] // 3
    x = fold_rows(dot_low(left, right, NT), k)
    return x[:, :k] + (x[:, k:2 * k] + x[:, 2 * k:])


def factor_parts(inverse):
    k = inverse.shape[0]
    parts = split3(inverse)
    return jnp.concatenate([parts, parts, parts], axis=1)


def times(parts, right):
    return fold_rows(dot_low(parts, right, NN), parts.shape[0] // 3)


def inverse_factor(gram):
    k = gram.shape[0]
    panel = 4
    rows = lax.broadcasted_iota(jnp.int32, (k, k), 0)
    cols = lax.broadcasted_iota(jnp.int32, (k, k), 1)
    eye = jnp.where(rows == cols, 1.0, 0.0).astype(F32)
    work = jnp.concatenate([gram, eye], axis=1)
    count = k // 8
    shape = (8, 2 * k)
    blocks = [work[8 * i:8 * i + 8] for i in range(count)]
    sub = lax.broadcasted_iota(jnp.int32, shape, 0)
    pivots = [jnp.zeros(shape, F32) for _ in range(count)]
    for j in range(0, k, panel):
        own, at = j // 8, j % 8
        row = [jnp.broadcast_to(blocks[own][at + a:at + a + 1, :], shape) for a in range(panel)]
        column = [
            [jnp.broadcast_to(blocks[i][:, j + a:j + a + 1], shape) for i in range(own, count)]
            for a in range(panel)
        ]
        corner = {
            (b, a): jnp.broadcast_to(column[a][0][at + b:at + b + 1, :], shape)
            for a in range(panel) for b in range(a, panel)
        }
        scaled = []
        for a in range(panel):
            pivot = corner[a, a]
            pivots[own] = jnp.where(sub == at + a, pivot, pivots[own])
            inverse = 1.0 / pivot
            scaled.append(row[a] * inverse)
            factor = {b: corner[b, a] * inverse for b in range(a + 1, panel)}
            for b in range(a + 1, panel):
                for c in range(b, panel):
                    corner[c, b] = corner[c, b] - factor[b] * corner[c, a]
            for b in range(a + 1, panel):
                row[b] = row[b] - factor[b] * row[a]
                column[b] = [y - factor[b] * x for x, y in zip(column[a], column[b])]
        for i in range(own, count):
            change = column[0][i - own] * scaled[0]
            for a in range(1, panel):
                change = change + column[a][i - own] * scaled[a]
            value = blocks[i] - change
            if i == own:
                value = jnp.where(sub >= at + panel, value, blocks[i])
                for a in range(panel):
                    value = jnp.where(sub == at + a, row[a], value)
            blocks[i] = value
    done = [blocks[i] * (1.0 / jnp.sqrt(pivots[i])) for i in range(count)]
    return jnp.concatenate(done, axis=0)[:, k:]


def pack(x):
    k = x.shape[0]
    return jnp.concatenate([x[:k // 2], x[k // 2:]], axis=1)


def unpack(x):
    k = x.shape[1] // 2
    return jnp.concatenate([x[:, :k], x[:, k:]], axis=0)


def flip(x, mask):
    result, bit = x, 1
    while bit <= mask:
        if mask & bit:
            result = result + bit - 2 * bit * lax.rem(lax.div(x, bit), 2)
        bit *= 2
    return result


def kernel(
    n, m, points, s_hbm, land_hbm, pen_hbm, v_hbm, out_ref, ray_ref,
    land_ref, pen_ref, s_full, s_high, s_mid, t_high, t_mid, field0, field1, field2, lap_ref, v_split,
    cbuf, rs, zr, fin, g_in, gr, gz, g_out, plane, edge, halo,
    c_sem, s_sem, rs_s, rs_r, z_s, z_r, ag_s, ag_r, gr_s, gr_r, gz_s, gz_r, ga_s, ga_r, h_s, h_r,
):
    lat = lax.axis_index("lat")
    lon = lax.axis_index("lon")
    t_count, a_count, b_count = s_hbm.shape
    k = v_hbm.shape[0]
    fields = (field0, field1, field2)
    blocks = t_count // b_count
    pairs = blocks // 2
    per = n // blocks
    shard = k // per
    halves = 2
    part_rows = shard // halves
    wide = 2 * b_count
    half_rows = a_count // 2
    gram_rows = k // blocks
    edge_groups = b_count // (2 * a_count)
    edge_rows = k // edge_groups
    inverse_points = 1.0 / points
    own_block = lax.div(lat, per)
    own_piece = lax.rem(lat, per)
    even = lax.rem(own_block, 2) == 0
    chip = lax.div(own_block, 2)

    def part(a):
        return pl.ds(a * b_count, b_count)

    def pair_rows(i):
        return pl.ds(pl.multiple_of(flip(chip, i) * wide, wide), wide)

    def piece_rows(piece, h=None):
        if h is None:
            return pl.ds(pl.multiple_of(piece * shard, shard), shard)
        return pl.ds(pl.multiple_of(piece * shard + h * part_rows, part_rows), part_rows)

    order = list(reversed(range(pairs)))
    groups = [order[g:g + 2] for g in range(0, pairs, 2)]
    land_copy = pltpu.make_async_copy(land_hbm, land_ref, c_sem.at[0])
    pen_copy = pltpu.make_async_copy(pen_hbm, pen_ref, c_sem.at[1])
    v_copies = [
        pltpu.make_async_copy(v_hbm.at[:, a, :], lap_ref.at[:, part(a)], c_sem.at[2])
        for a in range(a_count)
    ]
    s_copies = [
        [
            pltpu.make_async_copy(
                s_hbm.at[pair_rows(i), a, :], s_full.at[pair_rows(i), part(a)], s_sem.at[i, a // half_rows]
            )
            for a in range(a_count)
        ]
        for i in range(pairs)
    ]
    land_copy.start()
    for copy in v_copies:
        copy.start()
    for group in groups:
        for h in range(2):
            for i in group:
                for copy in s_copies[i][h * half_rows:(h + 1) * half_rows]:
                    copy.start()
    pen_copy.start()

    barrier = pltpu.get_barrier_semaphore()
    for d in range(1, n):
        pl.semaphore_signal(barrier, inc=1, device_id=(flip(lat, d), lon), device_id_type=MESH)
    for e in range(1, m):
        pl.semaphore_signal(barrier, inc=1, device_id=(lat, flip(lon, e)), device_id_type=MESH)

    def send(src, dst, s_s, s_r, where):
        copy = pltpu.make_async_remote_copy(
            src_ref=src, dst_ref=dst, send_sem=s_s, recv_sem=s_r,
            device_id=where, device_id_type=MESH,
        )
        copy.start()

    def arrived(ref, sem):
        pltpu.make_async_copy(ref, ref, sem).wait()

    def to_lat(d):
        return (flip(lat, d), lon)

    def to_lon(e):
        return (lat, flip(lon, e))

    lane = lax.broadcasted_iota(jnp.int32, (k, b_count), 1)

    def mask_row(a):
        return land_ref[a:a + 1, :].astype(F32)

    def start_halo(r):
        x = fields[r]
        packed = jnp.zeros((k, b_count), F32)
        for a in range(a_count):
            block = x[:, a * b_count:(a + 1) * b_count]
            low = block if a == 0 else pltpu.roll(block, a, axis=1)
            high = pltpu.roll(block, a_count + a + 1, axis=1)
            packed = jnp.where(lane == a, low, packed)
            packed = jnp.where(lane == a_count + a, high, packed)
        narrow = packed[:edge_rows]
        for q in range(1, edge_groups):
            rows = packed[q * edge_rows:(q + 1) * edge_rows]
            narrow = narrow + pltpu.roll(rows, q * 2 * a_count, axis=1)
        edge[r] = narrow
        up, down = (lax.rem(lat + 1, n), lon), (lax.rem(lat + n - 1, n), lon)
        right, left = (lat, lax.rem(lon + 1, m)), (lat, lax.rem(lon + m - 1, m))
        first, second = pl.ds(0, k), pl.ds(k, k)
        third, fourth = pl.ds(2 * k, edge_rows), pl.ds(2 * k + edge_rows, edge_rows)
        send(x.at[:, part(a_count - 1)], halo.at[r, first], h_s.at[r], h_r.at[r], up)
        send(x.at[:, part(0)], halo.at[r, second], h_s.at[r], h_r.at[r], down)
        send(edge.at[r], halo.at[r, third], h_s.at[r], h_r.at[r], right)
        send(edge.at[r], halo.at[r, fourth], h_s.at[r], h_r.at[r], left)

    def widen(x):
        return jnp.concatenate(
            [x] + [
                pltpu.roll(x, b_count - q * 2 * a_count, axis=1) for q in range(1, edge_groups)
            ], axis=0,
        )

    def laplacian(r):
        arrived(halo.at[r], h_r.at[r])
        x = fields[r]
        above = jnp.where(lat > 0, halo[r, :k, :], 0.0)
        below = jnp.where(lat < n - 1, halo[r, k:2 * k, :], 0.0)
        west = jnp.where(lon > 0, widen(halo[r, 2 * k:2 * k + edge_rows, :]), 0.0)
        east = jnp.where(lon < m - 1, widen(halo[r, 2 * k + edge_rows:, :]), 0.0)
        for a in range(a_count):
            block = x[:, a * b_count:(a + 1) * b_count]
            up = above if a == 0 else x[:, (a - 1) * b_count:a * b_count]
            down = below if a == a_count - 1 else x[:, (a + 1) * b_count:(a + 2) * b_count]
            left = jnp.where(
                lane == 0, pltpu.roll(west, b_count - a_count - a, axis=1),
                pltpu.roll(block, 1, axis=1),
            )
            right = jnp.where(
                lane == b_count - 1, pltpu.roll(east, b_count - 1 - a, axis=1),
                pltpu.roll(block, b_count - 1, axis=1),
            )
            total = (down + up + right + left) - 4.0 * block
            lap_ref[:, a * b_count:(a + 1) * b_count] = total * pen_ref[a:a + 1, :]

    def store_field(r, a, value):
        x = value * mask_row(a)
        at = slice(a * b_count, (a + 1) * b_count)
        fields[r][:, at] = x
        v_split[:, at] = split3(x)

    def store_pair(r, i, both, rest):
        value = both[:k] + (both[k:] + rest)
        low, up = value[:, :b_count], value[:, b_count:]
        cbuf[r, 2 * i] = jnp.where(even, low, up)
        cbuf[r, 2 * i + 1] = jnp.where(even, up, low)

    def project_first(group):
        sums = {}
        for h in range(2):
            at = slice(h * half_rows * b_count, (h + 1) * half_rows * b_count)
            for i in group:
                cols = pl.ds(h * half_rows * b_count, half_rows * b_count)
                arrived(s_full.at[pair_rows(i), cols], s_sem.at[i, h])
            for i in group:
                rows = pair_rows(i)
                high, mid = split(s_full[rows, at])
                s_high[rows, at] = high
                s_mid[rows, at] = mid
                both = dot_low(v_split[:2 * k, at], high, NT)
                rest = dot_low(v_split[:k, at], mid, NT)
                if h:
                    store_pair(0, i, sums[i][0] + both, sums[i][1] + rest)
                else:
                    sums[i] = both, rest

    def project_pair(r, i):
        rows = pair_rows(i)
        both = dot_low(v_split[:2 * k, :], t_high[:, rows], NN)
        rest = dot_low(v_split[:k, :], t_mid[:, rows], NN)
        store_pair(r, i, both, rest)

    def turn(source, target):
        for i in range(pairs):
            rows = slice(i * wide, (i + 1) * wide)
            for block in range(a_count // 2):
                at = slice(block * wide, (block + 1) * wide)
                target[at, rows] = source[rows, at].T

    def send_pair(r, i):
        for e in (1, 0):
            for q in range(per):
                d = (2 * i + e) * per + q
                if d:
                    rows = piece_rows(lax.rem(flip(lat, d), per))
                    send(
                        cbuf.at[r, 2 * i + e, rows], rs.at[r, d],
                        rs_s.at[r], rs_r.at[r], to_lat(d),
                    )

    def project(r):
        for group in groups:
            for i in group:
                project_pair(r, i)
            for i in group:
                send_pair(r, i)

    def finish_scatter(r):
        arrived(rs.at[r, pl.ds(1, n - 1)], rs_r.at[r])
        for h in range(halves):
            total = cbuf[r, 0, piece_rows(own_piece, h), :]
            at = slice(h * part_rows, (h + 1) * part_rows)
            for d in range(1, n):
                total = total + rs[r, d, at, :]
            zr[r, lon, at, :] = total
            own = zr.at[r, lon, pl.ds(h * part_rows, part_rows)]
            for e in reversed(range(1, m)):
                send(own, own, z_s.at[r], z_r.at[r, h], to_lon(e))

    def finish_lon(r, h):
        arrived(zr.at[r, pl.ds(1, m - 1), pl.ds(h * part_rows, part_rows)], z_r.at[r, h])
        at = slice(h * part_rows, (h + 1) * part_rows)
        total = zr[r, 0, at, :]
        for e in range(1, m):
            total = total + zr[r, e, at, :]
        fin[r, own_piece, at, :] = total

    def start_gather(r):
        for h in range(halves):
            finish_lon(r, h)
            rows = pl.ds(h * part_rows, part_rows)
            for d in reversed(range(1, n)):
                block = d // per
                send(
                    fin.at[r, own_piece, rows], fin.at[r, block * per + own_piece, rows],
                    ag_s.at[r], ag_r.at[r, block // 2], to_lat(d),
                )

    def wait_pair(r, i):
        if i:
            arrived(fin.at[r, pl.ds(2 * i * per, 2 * per)], ag_r.at[r, i])
        else:
            arrived(fin.at[r, pl.ds(1, 2 * per - 1)], ag_r.at[r, i])

    def load_block(r, block):
        return fin[r, block * per:(block + 1) * per].reshape(k, b_count)

    def gram_piece(block):
        return pl.ds(pl.multiple_of(block * gram_rows, gram_rows), gram_rows)

    def start_gram(r, value):
        g_in[r] = jnp.concatenate([value, value], axis=1)
        gr[r, lat] = g_in[r, gram_piece(own_block), :]
        for d in reversed(range(1, n)):
            send(
                g_in.at[r, gram_piece(flip(own_block, d // per))], gr.at[r, lat],
                gr_s.at[r], gr_r.at[r], to_lat(d),
            )

    def middle_gram(r):
        arrived(gr.at[r, pl.ds(1, n - 1)], gr_r.at[r])
        total = gr[r, 0]
        for d in range(1, n):
            total = total + gr[r, d]
        gz[r, lon] = total
        for e in reversed(range(1, m)):
            send(gz.at[r, lon], gz.at[r, lon], gz_s.at[r], gz_r.at[r], to_lon(e))

    def sum_gram(r):
        arrived(gz.at[r, pl.ds(1, m - 1)], gz_r.at[r])
        total = gz[r, 0]
        for e in range(1, m):
            total = total + gz[r, e]
        return total

    def spread_gram(r):
        rows = gram_piece(own_block)
        g_out[r, rows, :] = sum_gram(r)
        for block in reversed(range(1, blocks)):
            send(
                g_out.at[r, rows], g_out.at[r, rows], ga_s.at[r], ga_r.at[r], to_lat(block * per)
            )

    def other_pieces(r):
        return g_out.at[r, pl.ds(gram_rows, k - gram_rows)]

    def finish_gram(r):
        arrived(other_pieces(r), ga_r.at[r])
        return g_out[r, :, :k]

    def start_plane(value):
        plane[lat] = value
        for d in reversed(range(1, n)):
            send(plane.at[lat], plane.at[lat], c_sem.at[3], c_sem.at[4], to_lat(d))

    def finish_plane():
        arrived(plane.at[pl.ds(1, n - 1)], c_sem.at[4])
        total = plane[0]
        for d in range(1, n):
            total = total + plane[d]
        return total

    def expand_pair(r, i, parts=None):
        wait_pair(r - 1, i)
        near, far = load_block(r - 1, 2 * i), load_block(r - 1, 2 * i + 1)
        coeffs = jnp.concatenate(
            [jnp.where(even, near, far), jnp.where(even, far, near)], axis=1
        )
        high, mid = split(coeffs * inverse_points)
        stacked = jnp.concatenate([high, mid], axis=0)
        rows = pair_rows(i)
        for block in range(a_count // 2):
            at = slice(block * wide, (block + 1) * wide)
            both = dot_low(stacked, s_high[rows, at], NN)
            rest = dot_low(high, s_mid[rows, at], NN)
            value = lap_ref[:, at] + (both[:k] + (both[k:] + rest))
            if i < pairs - 1:
                lap_ref[:, at] = value
            else:
                if parts is not None:
                    value = times(parts, split3(value))
                store_field(r, 2 * block, value[:, :b_count])
                store_field(r, 2 * block + 1, value[:, b_count:])

    def gram():
        return products(v_split[...], v_split[...]) * inverse_points

    land_copy.wait()
    arrived(lap_ref, c_sem.at[2])
    for a in range(a_count):
        store_field(0, a, lap_ref[:, a * b_count:(a + 1) * b_count])
    project_first(groups[0])
    pl.semaphore_wait(barrier, n + m - 2)
    for i in groups[0]:
        send_pair(0, i)
    for group in groups[1:]:
        project_first(group)
        for i in group:
            send_pair(0, i)
    start_halo(0)
    pen_copy.wait()
    turn(s_high, t_high)
    finish_scatter(0)
    turn(s_mid, t_mid)
    laplacian(0)
    start_gather(0)
    for i in range(pairs):
        expand_pair(1, i)

    start_gram(0, gram())
    project(1)
    start_halo(1)
    middle_gram(0)
    finish_scatter(1)
    spread_gram(0)
    laplacian(1)
    start_gather(1)
    expand_pair(2, 0)
    parts = factor_parts(inverse_factor(finish_gram(0)))
    for i in range(1, pairs):
        expand_pair(2, i, parts)

    start_gram(1, gram())
    start_halo(2)
    project(2)
    middle_gram(1)
    laplacian(2)
    start_gram(2, products(v_split[...], split3(lap_ref[...])))
    finish_scatter(2)
    spread_gram(1)
    middle_gram(2)
    rows = gram_piece(own_block)
    if per == 1:
        for h in range(halves):
            finish_lon(2, h)
        coeffs = split3(load_block(2, 0))
        middle = products(coeffs, coeffs) * inverse_points
        g_out[2] = jnp.concatenate([middle, middle], axis=1)
    else:
        g_out[2] = jnp.zeros((k, b_count), F32)
        start_gather(2)
    rough = jnp.where(own_piece == 0, sum_gram(2), 0.0)
    g_out[2, rows, :] = g_out[2, rows, :] + rough
    start_plane(pack(g_out[2, :, :k]))
    inverse = inverse_factor(finish_gram(1))
    parts = factor_parts(inverse)
    for block in range(a_count // 2):
        at = slice(block * wide, (block + 1) * wide)
        out_ref[:, at] = times(parts, v_split[:, at])
    middle = unpack(finish_plane())
    if per > 1:
        for i in range(pairs):
            wait_pair(2, i)
        coeffs = split3(jnp.concatenate(
            [
                fin[2, pl.ds(flip(own_block, block) * per, per)].reshape(k, b_count)
                for block in range(blocks)
            ], axis=1,
        ))
        middle = middle + products(coeffs, coeffs) * inverse_points
    half = times(parts, split3(middle))
    ray_ref[...] = products(split3(half), split3(inverse)) * inverse_points
    arrived(plane.at[pl.ds(1, n - 1)], c_sem.at[3])
    for r in range(3):
        arrived(rs.at[r, pl.ds(1, n - 1)], rs_s.at[r])
        arrived(zr.at[r, pl.ds(1, m - 1)], z_s.at[r])
        arrived(gr.at[r, pl.ds(1, n - 1)], gr_s.at[r])
        arrived(gz.at[r, pl.ds(1, m - 1)], gz_s.at[r])
        arrived(halo.at[r], h_s.at[r])
        if r < 2 or per > 1:
            arrived(fin.at[r, pl.ds(1, n - 1)], ag_s.at[r])
        if r < 2:
            arrived(other_pieces(r), ga_s.at[r])


def write_out(x_ref, ray_ref, out_hbm, ray_hbm, sems):
    a_count, b_count = out_hbm.shape[1:]
    ray_copy = pltpu.make_async_copy(ray_ref, ray_hbm, sems.at[0])
    ray_copy.start()
    for a in range(a_count):
        at = pl.ds(a * b_count, b_count)
        pltpu.make_async_copy(x_ref.at[:, at], out_hbm.at[:, a, :], sems.at[1]).start()
    ray_copy.wait()
    pltpu.make_async_copy(x_ref, x_ref, sems.at[1]).wait()


def local(snapshots, land_sea, penalty, initial_basis):
    n, m = lax.axis_size("lat"), lax.axis_size("lon")
    t, a, b = snapshots.shape
    k = initial_basis.shape[0]
    points = float(a * b * n * m)
    p = a * b
    blocks = t // b
    shard = blocks * k // n
    sem = pltpu.SemaphoreType.DMA
    vmem = pltpu.VMEM
    any_spec = pl.BlockSpec(memory_space=pl.ANY)
    vmem_spec = pl.BlockSpec(memory_space=pltpu.VMEM)
    out, ray = pl.pallas_call(
        functools.partial(kernel, n, m, points),
        out_shape=(vmem((k, p), F32), vmem((k, k), F32)),
        in_specs=[any_spec, any_spec, any_spec, any_spec],
        out_specs=(vmem_spec, vmem_spec),
        scratch_shapes=[
            vmem((a, b), jnp.int32), vmem((a, b), F32),
            vmem((t, p), F32), vmem((t, p), BF16), vmem((t, p), BF16),
            vmem((p, t), BF16), vmem((p, t), BF16),
            vmem((k, p), F32), vmem((k, p), F32), vmem((k, p), F32),
            vmem((k, p), F32), vmem((3 * k, p), BF16),
            vmem((3, blocks, k, b), F32), vmem((3, n, shard, b), F32), vmem((3, m, shard, b), F32),
            vmem((3, n, shard, b), F32), vmem((3, k, b), F32), vmem((3, n, k // blocks, b), F32),
            vmem((3, m, k // blocks, b), F32), vmem((3, k, b), F32), vmem((n, k // 2, b), F32),
            vmem((3, 2 * a * k // b, b), F32), vmem((3, 2 * k + 4 * a * k // b, b), F32),
            sem((5,)), sem((blocks // 2, 2)),
            sem((3,)), sem((3,)), sem((3,)), sem((3, 2)), sem((3,)), sem((3, blocks // 2)),
            sem((3,)), sem((3,)), sem((3,)), sem((3,)), sem((2,)), sem((2,)), sem((3,)), sem((3,)),
        ],
        compiler_params=pltpu.CompilerParams(
            collective_id=0, has_side_effects=True, vmem_limit_bytes=60 * 1024 * 1024
        ),
        name="power_steps",
    )(snapshots, land_sea, penalty, initial_basis)
    return pl.pallas_call(
        write_out,
        out_shape=(jax.ShapeDtypeStruct((k, a, b), F32), jax.ShapeDtypeStruct((k, k), F32)),
        in_specs=[vmem_spec, vmem_spec],
        out_specs=(any_spec, any_spec),
        scratch_shapes=[sem((2,))],
        name="write_out",
    )(
        pltpu.with_memory_space_constraint(out, pltpu.VMEM),
        pltpu.with_memory_space_constraint(ray, pltpu.VMEM),
    )


def solution(mesh):
    in_specs = (P(None, "lat", "lon"), P("lat", "lon"), P("lat", "lon"), P(None, "lat", "lon"))
    out_specs = (P(None, "lat", "lon"), P())
    return jax.shard_map(local, mesh=mesh, in_specs=in_specs, out_specs=out_specs, check_vma=False)
```

```python
import functools

import jax
import jax.numpy as jnp
from jax import lax
from jax.experimental import pallas as pl
from jax.experimental.pallas import tpu as pltpu
from jax.sharding import PartitionSpec as P

STEPS = 2
MESH = pl.DeviceIdType.MESH
F32 = jnp.float32
BF16 = jnp.bfloat16
NT = (((1,), (1,)), ((), ()))
NN = (((1,), (0,)), ((), ()))


def dot_low(a, b, dims):
    return lax.dot_general(a, b, dims, preferred_element_type=F32)


def split(x):
    high = x.astype(BF16)
    return high, (x - high.astype(F32)).astype(BF16)


def split3(x):
    high = x.astype(BF16)
    rest = x - high.astype(F32)
    mid = rest.astype(BF16)
    return jnp.concatenate([high, mid, (rest - mid.astype(F32)).astype(BF16)], axis=0)


def fold_rows(x, k):
    return x[:k] + (x[k:2 * k] + x[2 * k:])


def products(left, right):
    k = left.shape[0] // 3
    x = fold_rows(dot_low(left, right, NT), k)
    return x[:, :k] + (x[:, k:2 * k] + x[:, 2 * k:])


def factor_parts(inverse):
    k = inverse.shape[0]
    parts = split3(inverse)
    return jnp.concatenate([parts, parts, parts], axis=1)


def times(parts, right):
    return fold_rows(dot_low(parts, right, NN), parts.shape[0] // 3)


def inverse_factor(gram):
    k = gram.shape[0]
    panel = 4
    rows = lax.broadcasted_iota(jnp.int32, (k, k), 0)
    cols = lax.broadcasted_iota(jnp.int32, (k, k), 1)
    eye = jnp.where(rows == cols, 1.0, 0.0).astype(F32)
    work = jnp.concatenate([gram, eye], axis=1)
    count = k // 8
    shape = (8, 2 * k)
    blocks = [work[8 * i:8 * i + 8] for i in range(count)]
    sub = lax.broadcasted_iota(jnp.int32, shape, 0)
    pivots = [jnp.zeros(shape, F32) for _ in range(count)]
    for j in range(0, k, panel):
        own, at = j // 8, j % 8
        row = [jnp.broadcast_to(blocks[own][at + a:at + a + 1, :], shape) for a in range(panel)]
        column = [
            [jnp.broadcast_to(blocks[i][:, j + a:j + a + 1], shape) for i in range(own, count)]
            for a in range(panel)
        ]
        corner = {
            (b, a): jnp.broadcast_to(column[a][0][at + b:at + b + 1, :], shape)
            for a in range(panel) for b in range(a, panel)
        }
        scaled = []
        for a in range(panel):
            pivot = corner[a, a]
            pivots[own] = jnp.where(sub == at + a, pivot, pivots[own])
            inverse = 1.0 / pivot
            scaled.append(row[a] * inverse)
            factor = {b: corner[b, a] * inverse for b in range(a + 1, panel)}
            for b in range(a + 1, panel):
                for c in range(b, panel):
                    corner[c, b] = corner[c, b] - factor[b] * corner[c, a]
            for b in range(a + 1, panel):
                row[b] = row[b] - factor[b] * row[a]
                column[b] = [y - factor[b] * x for x, y in zip(column[a], column[b])]
        for i in range(own, count):
            change = column[0][i - own] * scaled[0]
            for a in range(1, panel):
                change = change + column[a][i - own] * scaled[a]
            value = blocks[i] - change
            if i == own:
                value = jnp.where(sub >= at + panel, value, blocks[i])
                for a in range(panel):
                    value = jnp.where(sub == at + a, row[a], value)
            blocks[i] = value
    done = [blocks[i] * (1.0 / jnp.sqrt(pivots[i])) for i in range(count)]
    return jnp.concatenate(done, axis=0)[:, k:]


def pack(x):
    k = x.shape[0]
    return jnp.concatenate([x[:k // 2], x[k // 2:]], axis=1)


def unpack(x):
    k = x.shape[1] // 2
    return jnp.concatenate([x[:, :k], x[:, k:]], axis=0)


def flip(x, mask):
    result, bit = x, 1
    while bit <= mask:
        if mask & bit:
            result = result + bit - 2 * bit * lax.rem(lax.div(x, bit), 2)
        bit *= 2
    return result


def kernel(
    n, m, points, s_hbm, land_hbm, pen_hbm, v_hbm, out_ref, ray_ref,
    land_ref, pen_ref, s_full, s_high, s_mid, t_high, t_mid, field0, field1, field2, lap_ref, v_split,
    cbuf, rs, zr, fin, g_in, gr, gz, g_out, plane, edge, halo,
    c_sem, s_sem, out_sem, rs_r, z_r, ag_r, gr_r, gz_r, ga_r, h_r,
):
    lat = lax.axis_index("lat")
    lon = lax.axis_index("lon")
    t_count, a_count, b_count = s_hbm.shape
    k = v_hbm.shape[0]
    fields = (field0, field1, field2)
    blocks = t_count // b_count
    pairs = blocks // 2
    per = n // blocks
    shard = k // per
    halves = 2
    part_rows = shard // halves
    wide = 2 * b_count
    half_rows = a_count // 2
    gram_rows = k // blocks
    edge_groups = b_count // (2 * a_count)
    edge_rows = k // edge_groups
    inverse_points = 1.0 / points
    own_block = lax.div(lat, per)
    own_piece = lax.rem(lat, per)
    even = lax.rem(own_block, 2) == 0
    chip = lax.div(own_block, 2)

    def part(a):
        return pl.ds(a * b_count, b_count)

    def pair_rows(i):
        return pl.ds(pl.multiple_of(flip(chip, i) * wide, wide), wide)

    def piece_rows(piece, h=None):
        if h is None:
            return pl.ds(pl.multiple_of(piece * shard, shard), shard)
        return pl.ds(pl.multiple_of(piece * shard + h * part_rows, part_rows), part_rows)

    order = list(reversed(range(pairs)))
    groups = [order[g:g + 2] for g in range(0, pairs, 2)]
    land_copy = pltpu.make_async_copy(land_hbm, land_ref, c_sem.at[0])
    pen_copy = pltpu.make_async_copy(pen_hbm, pen_ref, c_sem.at[1])
    v_copies = [
        pltpu.make_async_copy(v_hbm.at[:, a, :], lap_ref.at[:, part(a)], c_sem.at[2])
        for a in range(a_count)
    ]
    s_copies = [
        [
            pltpu.make_async_copy(
                s_hbm.at[pair_rows(i), a, :], s_full.at[pair_rows(i), part(a)], s_sem.at[i, a // half_rows]
            )
            for a in range(a_count)
        ]
        for i in range(pairs)
    ]
    land_copy.start()
    for copy in v_copies:
        copy.start()
    for group in groups:
        for h in range(2):
            for i in group:
                for copy in s_copies[i][h * half_rows:(h + 1) * half_rows]:
                    copy.start()
    pen_copy.start()

    barrier = pltpu.get_barrier_semaphore()
    for d in range(1, n):
        pl.semaphore_signal(barrier, inc=1, device_id=(flip(lat, d), lon), device_id_type=MESH)
    for e in range(1, m):
        pl.semaphore_signal(barrier, inc=1, device_id=(lat, flip(lon, e)), device_id_type=MESH)

    def send(src, dst, s_s, s_r, where):
        copy = pltpu.make_async_remote_copy(
            src_ref=src, dst_ref=dst, send_sem=s_s, recv_sem=s_r,
            device_id=where, device_id_type=MESH,
        )
        copy.start()

    def arrived(ref, sem):
        pltpu.make_async_copy(ref, ref, sem).wait()

    def to_lat(d):
        return (flip(lat, d), lon)

    def to_lon(e):
        return (lat, flip(lon, e))

    lane = lax.broadcasted_iota(jnp.int32, (k, b_count), 1)

    def mask_row(a):
        return land_ref[a:a + 1, :].astype(F32)

    def start_halo(r):
        x = fields[r]
        packed = jnp.zeros((k, b_count), F32)
        for a in range(a_count):
            block = x[:, a * b_count:(a + 1) * b_count]
            low = block if a == 0 else pltpu.roll(block, a, axis=1)
            high = pltpu.roll(block, a_count + a + 1, axis=1)
            packed = jnp.where(lane == a, low, packed)
            packed = jnp.where(lane == a_count + a, high, packed)
        narrow = packed[:edge_rows]
        for q in range(1, edge_groups):
            rows = packed[q * edge_rows:(q + 1) * edge_rows]
            narrow = narrow + pltpu.roll(rows, q * 2 * a_count, axis=1)
        edge[r] = narrow
        up, down = (lax.rem(lat + 1, n), lon), (lax.rem(lat + n - 1, n), lon)
        right, left = (lat, lax.rem(lon + 1, m)), (lat, lax.rem(lon + m - 1, m))
        first, second = pl.ds(0, k), pl.ds(k, k)
        third, fourth = pl.ds(2 * k, edge_rows), pl.ds(2 * k + edge_rows, edge_rows)
        send(x.at[:, part(a_count - 1)], halo.at[r, first], out_sem.at[6], h_r.at[r], up)
        send(x.at[:, part(0)], halo.at[r, second], out_sem.at[6], h_r.at[r], down)
        send(edge.at[r], halo.at[r, third], out_sem.at[6], h_r.at[r], right)
        send(edge.at[r], halo.at[r, fourth], out_sem.at[6], h_r.at[r], left)

    def widen(x):
        return jnp.concatenate(
            [x] + [
                pltpu.roll(x, b_count - q * 2 * a_count, axis=1) for q in range(1, edge_groups)
            ], axis=0,
        )

    def laplacian(r):
        arrived(halo.at[r], h_r.at[r])
        x = fields[r]
        above = jnp.where(lat > 0, halo[r, :k, :], 0.0)
        below = jnp.where(lat < n - 1, halo[r, k:2 * k, :], 0.0)
        west = jnp.where(lon > 0, widen(halo[r, 2 * k:2 * k + edge_rows, :]), 0.0)
        east = jnp.where(lon < m - 1, widen(halo[r, 2 * k + edge_rows:, :]), 0.0)
        for a in range(a_count):
            block = x[:, a * b_count:(a + 1) * b_count]
            up = above if a == 0 else x[:, (a - 1) * b_count:a * b_count]
            down = below if a == a_count - 1 else x[:, (a + 1) * b_count:(a + 2) * b_count]
            left = jnp.where(
                lane == 0, pltpu.roll(west, b_count - a_count - a, axis=1),
                pltpu.roll(block, 1, axis=1),
            )
            right = jnp.where(
                lane == b_count - 1, pltpu.roll(east, b_count - 1 - a, axis=1),
                pltpu.roll(block, b_count - 1, axis=1),
            )
            total = (down + up + right + left) - 4.0 * block
            lap_ref[:, a * b_count:(a + 1) * b_count] = total * pen_ref[a:a + 1, :]

    def store_field(r, a, value):
        x = value * mask_row(a)
        at = slice(a * b_count, (a + 1) * b_count)
        fields[r][:, at] = x
        v_split[:, at] = split3(x)

    def store_pair(r, i, both, rest):
        value = both[:k] + (both[k:] + rest)
        low, up = value[:, :b_count], value[:, b_count:]
        cbuf[r, 2 * i] = jnp.where(even, low, up)
        cbuf[r, 2 * i + 1] = jnp.where(even, up, low)

    def project_first(group):
        sums = {}
        for h in range(2):
            at = slice(h * half_rows * b_count, (h + 1) * half_rows * b_count)
            for i in group:
                cols = pl.ds(h * half_rows * b_count, half_rows * b_count)
                arrived(s_full.at[pair_rows(i), cols], s_sem.at[i, h])
            for i in group:
                rows = pair_rows(i)
                high, mid = split(s_full[rows, at])
                s_high[rows, at] = high
                s_mid[rows, at] = mid
                both = dot_low(v_split[:2 * k, at], high, NT)
                rest = dot_low(v_split[:k, at], mid, NT)
                if h:
                    store_pair(0, i, sums[i][0] + both, sums[i][1] + rest)
                else:
                    sums[i] = both, rest

    def project_pair(r, i):
        rows = pair_rows(i)
        both = dot_low(v_split[:2 * k, :], t_high[:, rows], NN)
        rest = dot_low(v_split[:k, :], t_mid[:, rows], NN)
        store_pair(r, i, both, rest)

    def turn(source, target):
        for i in range(pairs):
            rows = slice(i * wide, (i + 1) * wide)
            for block in range(a_count // 2):
                at = slice(block * wide, (block + 1) * wide)
                target[at, rows] = source[rows, at].T

    def send_pair(r, i):
        for e in (1, 0):
            for q in range(per):
                d = (2 * i + e) * per + q
                if d:
                    rows = piece_rows(lax.rem(flip(lat, d), per))
                    send(
                        cbuf.at[r, 2 * i + e, rows], rs.at[r, d],
                        out_sem.at[0], rs_r.at[r], to_lat(d),
                    )

    def project(r):
        for group in groups:
            for i in group:
                project_pair(r, i)
            for i in group:
                send_pair(r, i)

    def finish_scatter(r):
        arrived(rs.at[r, pl.ds(1, n - 1)], rs_r.at[r])
        for h in range(halves):
            total = cbuf[r, 0, piece_rows(own_piece, h), :]
            at = slice(h * part_rows, (h + 1) * part_rows)
            for d in range(1, n):
                total = total + rs[r, d, at, :]
            zr[r, lon, at, :] = total
            own = zr.at[r, lon, pl.ds(h * part_rows, part_rows)]
            for e in reversed(range(1, m)):
                send(own, own, out_sem.at[1], z_r.at[r, h], to_lon(e))

    def finish_lon(r, h):
        arrived(zr.at[r, pl.ds(1, m - 1), pl.ds(h * part_rows, part_rows)], z_r.at[r, h])
        at = slice(h * part_rows, (h + 1) * part_rows)
        total = zr[r, 0, at, :]
        for e in range(1, m):
            total = total + zr[r, e, at, :]
        fin[r, own_piece, at, :] = total

    def start_gather(r):
        for h in range(halves):
            finish_lon(r, h)
            rows = pl.ds(h * part_rows, part_rows)
            for d in reversed(range(1, n)):
                block = d // per
                send(
                    fin.at[r, own_piece, rows], fin.at[r, block * per + own_piece, rows],
                    out_sem.at[2], ag_r.at[r, block // 2], to_lat(d),
                )

    def wait_pair(r, i):
        if i:
            arrived(fin.at[r, pl.ds(2 * i * per, 2 * per)], ag_r.at[r, i])
        else:
            arrived(fin.at[r, pl.ds(1, 2 * per - 1)], ag_r.at[r, i])

    def load_block(r, block):
        return fin[r, block * per:(block + 1) * per].reshape(k, b_count)

    def gram_piece(block):
        return pl.ds(pl.multiple_of(block * gram_rows, gram_rows), gram_rows)

    def start_gram(r, value):
        g_in[r] = jnp.concatenate([value, value], axis=1)
        gr[r, lat] = g_in[r, gram_piece(own_block), :]
        for d in reversed(range(1, n)):
            send(
                g_in.at[r, gram_piece(flip(own_block, d // per))], gr.at[r, lat],
                out_sem.at[3], gr_r.at[r], to_lat(d),
            )

    def middle_gram(r):
        arrived(gr.at[r, pl.ds(1, n - 1)], gr_r.at[r])
        total = gr[r, 0]
        for d in range(1, n):
            total = total + gr[r, d]
        gz[r, lon] = total
        for e in reversed(range(1, m)):
            send(gz.at[r, lon], gz.at[r, lon], out_sem.at[4], gz_r.at[r], to_lon(e))

    def sum_gram(r):
        arrived(gz.at[r, pl.ds(1, m - 1)], gz_r.at[r])
        total = gz[r, 0]
        for e in range(1, m):
            total = total + gz[r, e]
        return total

    def spread_gram(r):
        rows = gram_piece(own_block)
        g_out[r, rows, :] = sum_gram(r)
        for block in reversed(range(1, blocks)):
            send(
                g_out.at[r, rows], g_out.at[r, rows], out_sem.at[5], ga_r.at[r], to_lat(block * per)
            )

    def other_pieces(r):
        return g_out.at[r, pl.ds(gram_rows, k - gram_rows)]

    def finish_gram(r):
        arrived(other_pieces(r), ga_r.at[r])
        return g_out[r, :, :k]

    def start_plane(value):
        plane[lat] = value
        for d in reversed(range(1, n)):
            send(plane.at[lat], plane.at[lat], out_sem.at[7], c_sem.at[3], to_lat(d))

    def finish_plane():
        arrived(plane.at[pl.ds(1, n - 1)], c_sem.at[3])
        total = plane[0]
        for d in range(1, n):
            total = total + plane[d]
        return total

    def expand_pair(r, i, parts=None):
        wait_pair(r - 1, i)
        near, far = load_block(r - 1, 2 * i), load_block(r - 1, 2 * i + 1)
        coeffs = jnp.concatenate(
            [jnp.where(even, near, far), jnp.where(even, far, near)], axis=1
        )
        high, mid = split(coeffs * inverse_points)
        stacked = jnp.concatenate([high, mid], axis=0)
        rows = pair_rows(i)
        for block in range(a_count // 2):
            at = slice(block * wide, (block + 1) * wide)
            both = dot_low(stacked, s_high[rows, at], NN)
            rest = dot_low(high, s_mid[rows, at], NN)
            value = lap_ref[:, at] + (both[:k] + (both[k:] + rest))
            if i < pairs - 1:
                lap_ref[:, at] = value
            else:
                if parts is not None:
                    value = times(parts, split3(value))
                store_field(r, 2 * block, value[:, :b_count])
                store_field(r, 2 * block + 1, value[:, b_count:])

    def gram():
        return products(v_split[...], v_split[...]) * inverse_points

    land_copy.wait()
    arrived(lap_ref, c_sem.at[2])
    for a in range(a_count):
        store_field(0, a, lap_ref[:, a * b_count:(a + 1) * b_count])
    project_first(groups[0])
    pl.semaphore_wait(barrier, n + m - 2)
    for i in groups[0]:
        send_pair(0, i)
    for group in groups[1:]:
        project_first(group)
        for i in group:
            send_pair(0, i)
    start_halo(0)
    pen_copy.wait()
    turn(s_high, t_high)
    finish_scatter(0)
    turn(s_mid, t_mid)
    laplacian(0)
    start_gather(0)
    for i in range(pairs):
        expand_pair(1, i)

    start_gram(0, gram())
    project(1)
    start_halo(1)
    middle_gram(0)
    finish_scatter(1)
    spread_gram(0)
    laplacian(1)
    start_gather(1)
    expand_pair(2, 0)
    parts = factor_parts(inverse_factor(finish_gram(0)))
    for i in range(1, pairs):
        expand_pair(2, i, parts)

    start_gram(1, gram())
    start_halo(2)
    project(2)
    middle_gram(1)
    laplacian(2)
    start_gram(2, products(v_split[...], split3(lap_ref[...])))
    finish_scatter(2)
    spread_gram(1)
    middle_gram(2)
    if per == 1:
        for h in range(halves):
            finish_lon(2, h)
        coeffs = split3(load_block(2, 0))
        start_plane(pack(products(coeffs, coeffs) * inverse_points))
    else:
        start_gather(2)
    spread_gram(2)
    inverse = inverse_factor(finish_gram(1))
    parts = factor_parts(inverse)
    turned = split3(inverse.T)
    for block in range(a_count // 2):
        at = slice(block * wide, (block + 1) * wide)
        out_ref[:, at] = times(parts, v_split[:, at])
    if per == 1:
        middle = unpack(finish_plane())
    else:
        for i in range(pairs):
            wait_pair(2, i)
        coeffs = split3(jnp.concatenate(
            [
                fin[2, pl.ds(flip(own_block, block) * per, per)].reshape(k, b_count)
                for block in range(blocks)
            ], axis=1,
        ))
        middle = products(coeffs, coeffs) * inverse_points
    middle = middle + finish_gram(2)
    half = factor_parts(times(parts, split3(middle)))
    ray_ref[...] = times(half, turned) * inverse_points
    gathers = 2
    if per == 1:
        arrived(plane.at[pl.ds(1, n - 1)], out_sem.at[7])
    else:
        gathers = 3
    arrived(rs.at[:, pl.ds(1, n - 1)], out_sem.at[0])
    arrived(zr.at[:, pl.ds(1, m - 1)], out_sem.at[1])
    arrived(fin.at[pl.ds(0, gathers), pl.ds(1, n - 1)], out_sem.at[2])
    arrived(gr.at[:, pl.ds(1, n - 1)], out_sem.at[3])
    arrived(gz.at[:, pl.ds(1, m - 1)], out_sem.at[4])
    arrived(g_out.at[:, pl.ds(gram_rows, k - gram_rows)], out_sem.at[5])
    arrived(halo, out_sem.at[6])


def write_out(x_ref, ray_ref, out_hbm, ray_hbm, sems):
    a_count, b_count = out_hbm.shape[1:]
    ray_copy = pltpu.make_async_copy(ray_ref, ray_hbm, sems.at[0])
    ray_copy.start()
    for a in range(a_count):
        at = pl.ds(a * b_count, b_count)
        pltpu.make_async_copy(x_ref.at[:, at], out_hbm.at[:, a, :], sems.at[1]).start()
    ray_copy.wait()
    pltpu.make_async_copy(x_ref, x_ref, sems.at[1]).wait()


def local(snapshots, land_sea, penalty, initial_basis):
    n, m = lax.axis_size("lat"), lax.axis_size("lon")
    t, a, b = snapshots.shape
    k = initial_basis.shape[0]
    points = float(a * b * n * m)
    p = a * b
    blocks = t // b
    shard = blocks * k // n
    sem = pltpu.SemaphoreType.DMA
    vmem = pltpu.VMEM
    any_spec = pl.BlockSpec(memory_space=pl.ANY)
    vmem_spec = pl.BlockSpec(memory_space=pltpu.VMEM)
    out, ray = pl.pallas_call(
        functools.partial(kernel, n, m, points),
        out_shape=(vmem((k, p), F32), vmem((k, k), F32)),
        in_specs=[any_spec, any_spec, any_spec, any_spec],
        out_specs=(vmem_spec, vmem_spec),
        scratch_shapes=[
            vmem((a, b), jnp.int32), vmem((a, b), F32),
            vmem((t, p), F32), vmem((t, p), BF16), vmem((t, p), BF16),
            vmem((p, t), BF16), vmem((p, t), BF16),
            vmem((k, p), F32), vmem((k, p), F32), vmem((k, p), F32),
            vmem((k, p), F32), vmem((3 * k, p), BF16),
            vmem((3, blocks, k, b), F32), vmem((3, n, shard, b), F32), vmem((3, m, shard, b), F32),
            vmem((3, n, shard, b), F32), vmem((3, k, b), F32), vmem((3, n, k // blocks, b), F32),
            vmem((3, m, k // blocks, b), F32), vmem((3, k, b), F32), vmem((n, k // 2, b), F32),
            vmem((3, 2 * a * k // b, b), F32), vmem((3, 2 * k + 4 * a * k // b, b), F32),
            sem((4,)), sem((blocks // 2, 2)), sem((8,)), sem((3,)), sem((3, 2)),
            sem((3, blocks // 2)), sem((3,)), sem((3,)), sem((3,)), sem((3,)),
        ],
        compiler_params=pltpu.CompilerParams(
            collective_id=0, has_side_effects=True, vmem_limit_bytes=60 * 1024 * 1024
        ),
        name="power_steps",
    )(snapshots, land_sea, penalty, initial_basis)
    return pl.pallas_call(
        write_out,
        out_shape=(jax.ShapeDtypeStruct((k, a, b), F32), jax.ShapeDtypeStruct((k, k), F32)),
        in_specs=[vmem_spec, vmem_spec],
        out_specs=(any_spec, any_spec),
        scratch_shapes=[sem((2,))],
        name="write_out",
    )(
        pltpu.with_memory_space_constraint(out, pltpu.VMEM),
        pltpu.with_memory_space_constraint(ray, pltpu.VMEM),
    )


def solution(mesh):
    in_specs = (P(None, "lat", "lon"), P("lat", "lon"), P("lat", "lon"), P(None, "lat", "lon"))
    out_specs = (P(None, "lat", "lon"), P())
    return jax.shard_map(local, mesh=mesh, in_specs=in_specs, out_specs=out_specs, check_vma=False)
```
